32 devices in a mesh: replica: 4 (over y, x), shard: 8 (over z, core).
Axes of the slice: x: 2, y: 2, z: 4, core: 2. Of those that a mesh axis runs over, the one named last changes fastest.
Arguments:
- tokens: bfloat16 [8192, 2304], P(('replica', 'shard')), may hold values from -6 to 6
- w_query: bfloat16 [2304, 2048], P('shard'), may hold values from -0.375 to 0.375
- w_key: bfloat16 [2304, 1024], P('shard'), may hold values from -0.125 to 0.125
- w_value: bfloat16 [2304, 1024], P('shard'), may hold values from -0.125 to 0.125
- w_output: bfloat16 [2048, 2304], P('shard'), may hold values from -0.125 to 0.125
- gain_attn_in: bfloat16 [2304], P('shard'), may hold values from 0.25 to 1.75
- gain_attn_out: bfloat16 [2304], P('shard'), may hold values from 0.25 to 1.75
- gain_ffn_in: bfloat16 [2304], P('shard'), may hold values from 0.25 to 1.75
- gain_ffn_out: bfloat16 [2304], P('shard'), may hold values from 0.25 to 1.75
- w_gate: bfloat16 [9216, 2304], P('shard'), may hold values from -0.125 to 0.125
- w_up: bfloat16 [9216, 2304], P('shard'), may hold values from -0.125 to 0.125
- w_down: bfloat16 [9216, 2304], P('shard'), may hold values from -0.0625 to 0.0625
- segment_ids: int32 [4, 1024], P('replica'), may hold values from 0 to 3, never falling along the last dimension, each value on 1 to 384 neighbouring positions
- cotangent: bfloat16 [8192, 2304], P(('replica', 'shard')), may hold values from -6 to 6
Outputs:
- output: bfloat16 [8192, 2304], P(('replica', 'shard'))
- input_grad: float32 [8192, 2304], P(('replica', 'shard'))
- grad_query: float32 [2304, 2048], P('shard')
- grad_key: float32 [2304, 1024], P('shard')
- grad_value: float32 [2304, 1024], P('shard')
- grad_out_proj: float32 [2048, 2304], P('shard')
- grad_gain_attn_in: float32 [2304], P('shard')
- grad_gain_attn_out: float32 [2304], P('shard')
- grad_gain_ffn_in: float32 [2304], P('shard')
- grad_gain_ffn_out: float32 [2304], P('shard')
- grad_gate: float32 [9216, 2304], P('shard')
- grad_up: float32 [9216, 2304], P('shard')
- grad_down: float32 [9216, 2304], P('shard')
The draws below stay inside these ranges and needn't reach their ends.
Inputs may be any that keep to these rules, and one draw needn't show every extreme that they name: `segment_ids`: along a row the ids never fall; every continuation 0 to 3 has one to 384 tokens, and one has exactly 384.
All inputs are finite; a program needn't handle non-finite values.
Results may differ from the reference program's by a relative error of at most 0.028.
Values may be sent and summed in bfloat16 or wider, within the bound.
A program may use at most 320 MiB of HBM per device.

```python
import math
import jax
import jax.numpy as jnp
import numpy as np
from jax import lax

D = 2304
H = 8
KV = 4
HD = 256
FF = 9216
PROMPT = 1024
CONT_TOK = 1024
CONTS = 4
MOST_CONT = 384
GROUP_TOK = 2048
GROUPS = 4
TOKENS = 8192


def strengthened(values, own_key, source, target, blocks, factor):
    def block_of(axis_at):
        return (jnp.arange(values.shape[axis_at]) // (values.shape[axis_at] // blocks)).reshape((-1,) + (1,) * (values.ndim - 1 - axis_at))

    first = jax.random.permutation(own_key, blocks)[block_of(target)]
    second = (block_of(target) + blocks // 2) % blocks
    return jnp.where((block_of(source) == first) | (block_of(source) == second), factor * values, values)


def shard_levels(own_key, shape, cuts, low, high):
    def one(position, blocks):
        heights = jax.random.uniform(jax.random.fold_in(jax.random.fold_in(own_key, 6), position), (blocks,), jnp.float32, low / len(cuts), high / len(cuts))
        return jnp.repeat(jnp.exp(heights), shape[position] // blocks).reshape((-1,) + (1,) * (len(shape) - position - 1))

    level = one(*cuts[0])
    for cut in cuts[1:]:
        level = level * one(*cut)
    return level


def length_profile(number_of, total, reach, skew):
    weights = [(1 << 20) // math.isqrt(standing ** skew) + 1 for standing in range(2, number_of + 1)]
    rest, given = total - reach - (number_of - 1), [1] * (number_of - 1)
    while rest > 0:
        free = [i for i in range(number_of - 1) if given[i] < reach]
        pool, remaining = sum([weights[i] for i in free]), rest
        for i in free:
            addition = min(reach - given[i], max(1, remaining * weights[i] // pool), rest)
            given[i] = given[i] + addition
            rest = rest - addition
    return np.array([reach] + given)


def uneven_parts(rng, number_of, total, reach, slope):
    if number_of == 2:
        one = jax.random.randint(rng, (), max(1, total - reach), min(reach, total - 1) + 1)
        return jnp.stack([one, total - one])
    sizes = jnp.asarray(length_profile(number_of, total, reach, slope), jnp.int32)
    pairs = (number_of - 1) // 2
    source_of, taker = sizes[1:1 + 2 * pairs:2], sizes[2:2 + 2 * pairs:2]
    room = jnp.minimum(source_of - 1, reach - taker)
    moved = jax.random.randint(jax.random.fold_in(rng, 1), (pairs,), 0, 1 << 20) % (room + 1)
    sizes = sizes.at[1:1 + 2 * pairs:2].set(source_of - moved).at[2:2 + 2 * pairs:2].set(taker + moved)
    return sizes[jax.random.permutation(jax.random.fold_in(rng, 2), number_of)]


def normal_values(key, shape, scale, limit, shards=(), kind=jnp.bfloat16):
    loudness = shard_levels(key, shape, shards, -0.22, 0.18) if shards else 1.0
    array = jax.random.normal(key, shape, jnp.float32) * scale * loudness
    return jnp.minimum(jnp.maximum(array, -limit), limit).astype(kind)


def gaussian_with(stream_key, shape, spread, limit, cuts, heavy, held_as=jnp.bfloat16):
    values = spread * jax.random.normal(stream_key, shape, jnp.float32)
    if cuts:
        values = values * shard_levels(stream_key, shape, cuts, -0.22, 0.18)
    return jnp.clip(strengthened(values, jax.random.fold_in(stream_key, 3), *heavy), -limit, limit).astype(held_as)


def setup_inputs(seed: int = 0) -> dict:
    arg_keys = jax.random.split(jax.random.key(seed), 15)
    return {
        "tokens": gaussian_with(arg_keys[0], (TOKENS, D), 1.0, 6.0, ((0, 32),), (0, 1, 32, 2.75)),
        "w_query": normal_values(arg_keys[1], (D, H * HD), (D // 9) ** -0.5, 0.375, ((0, 8),)),
        "w_key": normal_values(arg_keys[2], (D, KV * HD), D ** -0.5, 0.125, ((0, 8),)),
        "w_value": normal_values(arg_keys[3], (D, KV * HD), D ** -0.5, 0.125, ((0, 8),)),
        "w_output": normal_values(arg_keys[4], (H * HD, D), (H * HD) ** -0.5, 0.125, ((0, 8),)),
        "gain_attn_in": jnp.clip(1.0 + 0.15 * jax.random.normal(arg_keys[5], (D,), jnp.float32), 0.25, 1.75).astype(jnp.bfloat16),
        "gain_attn_out": jnp.clip(1.0 + 0.15 * jax.random.normal(arg_keys[6], (D,), jnp.float32), 0.25, 1.75).astype(jnp.bfloat16),
        "gain_ffn_in": jnp.clip(1.0 + 0.15 * jax.random.normal(arg_keys[7], (D,), jnp.float32), 0.25, 1.75).astype(jnp.bfloat16),
        "gain_ffn_out": jnp.clip(1.0 + 0.15 * jax.random.normal(arg_keys[8], (D,), jnp.float32), 0.25, 1.75).astype(jnp.bfloat16),
        "w_gate": normal_values(arg_keys[9], (FF, D), D ** -0.5, 0.125, ((0, 8),)),
        "w_up": normal_values(arg_keys[10], (FF, D), D ** -0.5, 0.125, ((0, 8),)),
        "w_down": normal_values(arg_keys[11], (FF, D), FF ** -0.5, 0.0625, ((0, 8),)),
        "segment_ids": jax.vmap(lambda own: jnp.searchsorted(jnp.cumsum(uneven_parts(own, CONTS, CONT_TOK, MOST_CONT, 1)), jnp.arange(CONT_TOK), side="right"))(jax.random.split(arg_keys[12], GROUPS)).reshape((GROUPS, CONT_TOK)).astype(jnp.int32),
        "cotangent": normal_values(arg_keys[13], (TOKENS, D), 1.0, 6.0, ((0, 32),)),
    }


@jax.custom_vjp
def low(v):
    return lax.optimization_barrier(v.astype(jnp.bfloat16)).astype(jnp.float32)

@jax.custom_vjp
def low_back(v):
    return v

def low_keep(v):
    return (low(v), None)

def low_pass(kept, grad):
    return (grad,)

def back_keep(v):
    return (v, None)

def back_low(kept, grad):
    return (low(grad),)
low.defvjp(low_keep, low_pass)
low_back.defvjp(back_keep, back_low)
EPS = 1e-06
CAP = 50.0
THETA = 10000.0
NEGATIVE = -1e+30

def wide_dot(left, right):
    return jnp.dot(left, right, precision=lax.Precision.HIGHEST, preferred_element_type=jnp.float32)

def rms_scaled(values, gain):
    return values * lax.rsqrt(lax.optimization_barrier(jnp.mean(values * values, axis=-1, keepdims=True)) + EPS) * gain

def rotate(values, positions, head_count, head_dim):
    tok_count = values.shape[0]
    half = head_dim // 2
    rates = THETA ** (-(jnp.arange(half, dtype=jnp.float32) * 2.0) / head_dim)
    angles = positions.astype(jnp.float32)[:, None] * rates[None, :]
    cosine = jnp.cos(angles)[:, None, :]
    sine = jnp.sin(angles)[:, None, :]
    shaped = values.reshape(tok_count, head_count, head_dim)
    first = shaped[:, :, :half]
    second = shaped[:, :, half:]
    turned = jnp.concatenate([first * cosine - second * sine, second * cosine + first * sine], axis=-1)
    return turned.reshape(tok_count, head_count * head_dim)

def layout(segment_row):
    prompt_marks = jnp.full((PROMPT,), -1, dtype=jnp.int32)
    key_segments = jnp.concatenate([prompt_marks, segment_row.astype(jnp.int32)])
    earlier = lax.optimization_barrier(jnp.sum((segment_row[None, :] < key_segments[:, None]).astype(jnp.int32), axis=1))
    positions = jnp.arange(GROUP_TOK, dtype=jnp.int32) - earlier
    return (key_segments, positions)

def group_attention(queries, keys, values, key_segments):
    head_group = H // KV
    block = 512 if GROUP_TOK % 512 == 0 else GROUP_TOK
    key_index = jnp.arange(GROUP_TOK, dtype=jnp.int32)
    keys_shaped = keys.reshape(GROUP_TOK, KV, HD)
    values_shaped = values.reshape(GROUP_TOK, KV, HD)

    def one_block(pieces):
        query_block, query_index, query_segments = pieces
        shaped = query_block.reshape(block, KV, head_group, HD)
        scores = low_back(jnp.einsum('qkgd,pkd->kgqp', shaped, keys_shaped, precision=lax.Precision.HIGHEST))
        capped = CAP * jnp.tanh(scores / CAP)
        visible = (key_index[None, :] <= query_index[:, None]) & ((key_index[None, :] < PROMPT) | (key_segments[None, :] == query_segments[:, None]))
        capped = jnp.where(visible[None, None], capped, NEGATIVE)
        probs = jax.nn.softmax(capped, axis=-1)
        mixed = jnp.einsum('kgqp,pkd->qkgd', low(probs), values_shaped, precision=lax.Precision.HIGHEST)
        return mixed.reshape(block, H * HD)
    blocks = GROUP_TOK // block
    outputs = lax.map(jax.checkpoint(one_block), (queries.reshape(blocks, block, H * HD), key_index.reshape(blocks, block), key_segments.reshape(blocks, block)))
    return outputs.reshape(GROUP_TOK, H * HD)

def layer(x, w_query, w_key, w_value, w_output, gain_attn_in, gain_attn_out, gain_ffn_in, gain_ffn_out, w_gate, w_up, w_down, key_segments, positions):
    normed = low(rms_scaled(x, gain_attn_in))
    query_lin = low_back(wide_dot(normed, w_query))
    key_lin = low_back(wide_dot(normed, w_key))
    value_lin = low_back(wide_dot(normed, w_value))
    flat_positions = positions.reshape(-1)
    queries = low(rotate(query_lin, flat_positions, H, HD) * HD ** (-0.5))
    keys = low(rotate(key_lin, flat_positions, KV, HD))
    values = low(value_lin)

    def per_group(parts):
        return group_attention(parts[0], parts[1], parts[2], parts[3])
    attended = lax.map(per_group, (queries.reshape(GROUPS, GROUP_TOK, H * HD), keys.reshape(GROUPS, GROUP_TOK, KV * HD), values.reshape(GROUPS, GROUP_TOK, KV * HD), key_segments))
    attended = low(low_back(attended.reshape(TOKENS, H * HD)))
    raw_attn = low_back(wide_dot(attended, w_output))
    hidden_state = x + rms_scaled(raw_attn, gain_attn_out)
    normed_ffn = low(rms_scaled(hidden_state, gain_ffn_in))
    gate = low_back(wide_dot(normed_ffn, w_gate.T))
    up = low_back(wide_dot(normed_ffn, w_up.T))
    glu = low(jax.nn.gelu(gate, approximate=True) * up)
    raw_ffn = low_back(wide_dot(glu, w_down))
    return hidden_state + rms_scaled(raw_ffn, gain_ffn_out)

def reference(tokens, w_query, w_key, w_value, w_output, gain_attn_in, gain_attn_out, gain_ffn_in, gain_ffn_out, w_gate, w_up, w_down, segment_ids, cotangent):
    key_segments, positions = jax.vmap(layout)(segment_ids.astype(jnp.int32))
    floats = (tokens.astype(jnp.float32), w_query.astype(jnp.float32), w_key.astype(jnp.float32), w_value.astype(jnp.float32), w_output.astype(jnp.float32), gain_attn_in.astype(jnp.float32), gain_attn_out.astype(jnp.float32), gain_ffn_in.astype(jnp.float32), gain_ffn_out.astype(jnp.float32), w_gate.astype(jnp.float32), w_up.astype(jnp.float32), w_down.astype(jnp.float32))

    def forward(x, wq_all, wk_all, wv_all, wo_all, g_one, g_two, g_three, g_four, wg_all, wu_all, wd_all):
        return layer(x, wq_all, wk_all, wv_all, wo_all, g_one, g_two, g_three, g_four, wg_all, wu_all, wd_all, key_segments, positions)
    result, pull = jax.vjp(forward, *floats)
    grads = pull(cotangent.astype(jnp.float32))
    return (result.astype(jnp.bfloat16), grads[0], grads[1], grads[2], grads[3], grads[4], grads[5], grads[6], grads[7], grads[8], grads[9], grads[10], grads[11])
```

```python
import functools

import jax
import jax.numpy as jnp
from jax import lax
from jax.experimental import pallas as pl
from jax.experimental.pallas import tpu as pltpu
from jax.sharding import PartitionSpec as P

H = 8
KV = 4
HD = 256
PROMPT = 1024


EPS = 1e-06
CAP = 50.0
THETA = 10000.0
NEGATIVE = -1e30


def inv_rms(values):
    return lax.rsqrt(jnp.mean(values * values, axis=-1, keepdims=True) + EPS)


def rms_scaled(values, gain):
    return values * inv_rms(values) * gain


def rotate(values, positions, head_count, head_dim, sign):
    tok_count = values.shape[0]
    half = head_dim // 2
    rates = THETA ** (-(jnp.arange(half, dtype=jnp.float32) * 2.0) / head_dim)
    angles = positions.astype(jnp.float32)[:, None] * rates[None, :]
    cosine = jnp.cos(angles)[:, None, :]
    sine = sign * jnp.sin(angles)[:, None, :]
    shaped = values.reshape(tok_count, head_count, head_dim)
    first = shaped[:, :, :half]
    second = shaped[:, :, half:]
    turned = jnp.concatenate(
        [first * cosine - second * sine, second * cosine + first * sine], axis=-1
    )
    return turned.reshape(tok_count, head_count * head_dim)


def glu_value(gate, up):
    return jax.nn.gelu(gate, approximate=True) * up


def on_device(
    tokens,
    w_query,
    w_key,
    w_value,
    w_output,
    gain_attn_in,
    gain_attn_out,
    gain_ffn_in,
    gain_ffn_out,
    w_gate,
    w_up,
    w_down,
    segment_ids,
    cotangent,
):
    tok_rows = tokens.shape[0]
    query_cols = w_query.shape[1]
    kv_cols = w_key.shape[1]
    group_rows = tok_rows * lax.axis_size("shard")
    head_group = H // KV
    shard_index = lax.axis_index("shard")
    start_row = shard_index * tok_rows
    segment_row = segment_ids[0]
    key_segments = jnp.concatenate([jnp.full((PROMPT,), -1, jnp.int32), segment_row])
    key_index = jnp.arange(group_rows, dtype=jnp.int32)
    query_index = start_row + jnp.arange(tok_rows, dtype=jnp.int32)
    query_segments = lax.dynamic_slice_in_dim(key_segments, start_row, tok_rows)
    earlier = jnp.sum((segment_row[None, :] < query_segments[:, None]).astype(jnp.int32), axis=1)
    positions = query_index - earlier
    visible = (key_index[None, :] <= query_index[:, None]) & (
        (key_index[None, :] < PROMPT) | (key_segments[None, :] == query_segments[:, None])
    )
    gain_stack = jnp.stack([gain_attn_in, gain_attn_out, gain_ffn_in, gain_ffn_out])
    full_query, full_key, full_value, full_out, gains = (
        lax.all_gather(w_query, "shard", axis=0, tiled=True),
        lax.all_gather(w_key, "shard", axis=0, tiled=True),
        lax.all_gather(w_value, "shard", axis=0, tiled=True),
        lax.all_gather(w_output, "shard", axis=0, tiled=True),
        lax.all_gather(gain_stack, "shard", axis=1, tiled=True),
    )
    gain_first = gains[0].astype(jnp.float32)
    gain_second = gains[1].astype(jnp.float32)
    gain_third = gains[2].astype(jnp.float32)
    gain_fourth = gains[3].astype(jnp.float32)
    x_float = tokens.astype(jnp.float32)
    normed = rms_scaled(x_float, gain_first).astype(jnp.bfloat16)
    query_lin = jnp.dot(normed, full_query, preferred_element_type=jnp.float32)
    key_lin = jnp.dot(normed, full_key, preferred_element_type=jnp.float32)
    value_lin = jnp.dot(normed, full_value, preferred_element_type=jnp.float32)
    query_scale = HD ** (-0.5)
    queries = (rotate(query_lin, positions, H, HD, 1.0) * query_scale).astype(jnp.bfloat16)
    keys = rotate(key_lin, positions, KV, HD, 1.0).astype(jnp.bfloat16)
    values = value_lin.astype(jnp.bfloat16)
    group_keys, group_values = (
        lax.all_gather(keys, "shard", axis=0, tiled=True),
        lax.all_gather(values, "shard", axis=0, tiled=True),
    )
    keys_shaped = group_keys.reshape(group_rows, KV, HD)
    values_shaped = group_values.reshape(group_rows, KV, HD)
    query_shaped = queries.reshape(tok_rows, KV, head_group, HD)

    def capped_scores():
        scores = jnp.einsum(
            "qkgd,pkd->kgqp", query_shaped, keys_shaped, preferred_element_type=jnp.float32
        )
        bent = jnp.tanh(scores / CAP)
        return (bent, jnp.where(visible[None, None], CAP * bent, NEGATIVE))

    bent, capped = capped_scores()
    highest = jnp.max(capped, axis=-1, keepdims=True)
    log_total = highest + jnp.log(jnp.sum(jnp.exp(capped - highest), axis=-1, keepdims=True))
    probs = jnp.exp(capped - log_total)
    probs_low = probs.astype(jnp.bfloat16)
    attended = jnp.einsum(
        "kgqp,pkd->qkgd", probs_low, values_shaped, preferred_element_type=jnp.float32
    )
    attended_low = attended.reshape(tok_rows, query_cols).astype(jnp.bfloat16)
    raw_attn = jnp.dot(attended_low, full_out, preferred_element_type=jnp.float32)
    hidden_state = x_float + rms_scaled(raw_attn, gain_second)
    normed_ffn = rms_scaled(hidden_state, gain_third).astype(jnp.bfloat16)
    group_normed = lax.all_gather(normed_ffn, "shard", axis=0, tiled=True)
    gate = jnp.einsum("td,fd->tf", group_normed, w_gate, preferred_element_type=jnp.float32)
    up = jnp.einsum("td,fd->tf", group_normed, w_up, preferred_element_type=jnp.float32)
    glu = glu_value(gate, up).astype(jnp.bfloat16)
    raw_ffn = lax.psum_scatter(
        jnp.dot(glu, w_down, preferred_element_type=jnp.float32).astype(jnp.bfloat16),
        "shard",
        scatter_dimension=0,
        tiled=True,
    ).astype(jnp.float32)
    output = (hidden_state + rms_scaled(raw_ffn, gain_fourth)).astype(jnp.bfloat16)
    grad_top = cotangent.astype(jnp.float32)
    _, pull_fourth = jax.vjp(rms_scaled, raw_ffn, gain_fourth)
    d_raw_ffn, grad_gain_fourth = pull_fourth(grad_top)
    d_raw_low = d_raw_ffn.astype(jnp.bfloat16)
    group_d_raw = lax.all_gather(d_raw_low, "shard", axis=0, tiled=True)
    grad_down = jnp.einsum("tf,td->fd", glu, group_d_raw, preferred_element_type=jnp.float32)
    d_glu = jnp.einsum("td,fd->tf", group_d_raw, w_down, preferred_element_type=jnp.float32)
    _, pull_glu = jax.vjp(glu_value, gate, up)
    d_gate, d_up = pull_glu(d_glu)
    d_gate_low = d_gate.astype(jnp.bfloat16)
    d_up_low = d_up.astype(jnp.bfloat16)
    grad_gate = jnp.einsum(
        "tf,td->fd", d_gate_low, group_normed, preferred_element_type=jnp.float32
    )
    grad_up = jnp.einsum("tf,td->fd", d_up_low, group_normed, preferred_element_type=jnp.float32)
    gate_part = jnp.dot(d_gate_low, w_gate, preferred_element_type=jnp.float32)
    up_part = jnp.dot(d_up_low, w_up, preferred_element_type=jnp.float32)
    d_normed_ffn = lax.psum_scatter(
        (gate_part + up_part).astype(jnp.bfloat16), "shard", scatter_dimension=0, tiled=True
    ).astype(jnp.float32)
    _, pull_third = jax.vjp(rms_scaled, hidden_state, gain_third)
    d_hidden_part, grad_gain_third = pull_third(d_normed_ffn)
    d_hidden = grad_top + d_hidden_part
    _, pull_second = jax.vjp(rms_scaled, raw_attn, gain_second)
    d_raw_attn, grad_gain_second = pull_second(d_hidden)
    d_raw_attn_low = d_raw_attn.astype(jnp.bfloat16)
    picked = attended_low
    grad_out_proj = lax.psum_scatter(
        jnp.einsum("tf,td->fd", picked, d_raw_attn_low, preferred_element_type=jnp.float32).astype(
            jnp.bfloat16
        ),
        "shard",
        scatter_dimension=0,
        tiled=True,
    ).astype(jnp.float32)
    d_attended_low = jnp.einsum(
        "td,fd->tf", d_raw_attn_low, full_out, preferred_element_type=jnp.float32
    ).astype(jnp.bfloat16)
    d_attended_shaped = d_attended_low.reshape(tok_rows, KV, head_group, HD)
    bent_again, capped_again = capped_scores()
    probs_again = jnp.exp(capped_again - log_total)
    probs_again_low = probs_again.astype(jnp.bfloat16)
    d_probs = jnp.einsum(
        "qkgd,pkd->kgqp", d_attended_shaped, values_shaped, preferred_element_type=jnp.float32
    )
    d_capped = probs_again * (d_probs - jnp.sum(probs_again * d_probs, axis=-1, keepdims=True))
    d_scores_low = (d_capped * (1.0 - bent_again * bent_again)).astype(jnp.bfloat16)
    d_queries = jnp.einsum(
        "kgqp,pkd->qkgd", d_scores_low, keys_shaped, preferred_element_type=jnp.float32
    ).reshape(tok_rows, query_cols)
    d_keys_group = jnp.einsum(
        "kgqp,qkgd->pkd", d_scores_low, query_shaped, preferred_element_type=jnp.float32
    ).reshape(group_rows, kv_cols)
    d_values_group = jnp.einsum(
        "kgqp,qkgd->pkd", probs_again_low, d_attended_shaped, preferred_element_type=jnp.float32
    ).reshape(group_rows, kv_cols)
    d_keys, d_values = (
        lax.psum_scatter(
            d_keys_group.astype(jnp.bfloat16), "shard", scatter_dimension=0, tiled=True
        ).astype(jnp.float32),
        lax.psum_scatter(
            d_values_group.astype(jnp.bfloat16), "shard", scatter_dimension=0, tiled=True
        ).astype(jnp.float32),
    )
    d_query_low = rotate(d_queries * query_scale, positions, H, HD, -1.0).astype(jnp.bfloat16)
    d_key_low = rotate(d_keys, positions, KV, HD, -1.0).astype(jnp.bfloat16)
    d_value_low = d_values.astype(jnp.bfloat16)
    d_normed = jnp.einsum("tf,df->td", d_query_low, full_query, preferred_element_type=jnp.float32)
    d_normed = d_normed + jnp.einsum(
        "tf,df->td", d_key_low, full_key, preferred_element_type=jnp.float32
    )
    d_normed = d_normed + jnp.einsum(
        "tf,df->td", d_value_low, full_value, preferred_element_type=jnp.float32
    )
    _, pull_first = jax.vjp(rms_scaled, x_float, gain_first)
    d_input_part, grad_gain_first = pull_first(d_normed)
    input_grad = d_hidden + d_input_part
    d_projected = jnp.concatenate([d_query_low, d_key_low, d_value_low], axis=1)
    picked = normed
    grad_projected = lax.psum_scatter(
        jnp.einsum("tc,tf->cf", picked, d_projected, preferred_element_type=jnp.float32).astype(
            jnp.bfloat16
        ),
        "shard",
        scatter_dimension=0,
        tiled=True,
    ).astype(jnp.float32)
    grad_query = grad_projected[:, :query_cols]
    grad_key = grad_projected[:, query_cols : query_cols + kv_cols]
    grad_value = grad_projected[:, query_cols + kv_cols :]
    gain_terms = jnp.stack([grad_gain_first, grad_gain_second, grad_gain_third, grad_gain_fourth])
    gain_shares = lax.psum_scatter(
        gain_terms.astype(jnp.bfloat16), "shard", scatter_dimension=1, tiled=True
    ).astype(jnp.float32)
    grad_query, grad_key, grad_value, grad_out_proj, gain_shares, grad_gate, grad_up, grad_down = (
        lax.psum(grad_query.astype(jnp.bfloat16), "replica").astype(jnp.float32),
        lax.psum(grad_key.astype(jnp.bfloat16), "replica").astype(jnp.float32),
        lax.psum(grad_value.astype(jnp.bfloat16), "replica").astype(jnp.float32),
        lax.psum(grad_out_proj.astype(jnp.bfloat16), "replica").astype(jnp.float32),
        lax.psum(gain_shares.astype(jnp.bfloat16), "replica").astype(jnp.float32),
        lax.psum(grad_gate.astype(jnp.bfloat16), "replica").astype(jnp.float32),
        lax.psum(grad_up.astype(jnp.bfloat16), "replica").astype(jnp.float32),
        lax.psum(grad_down.astype(jnp.bfloat16), "replica").astype(jnp.float32),
    )
    return (
        output,
        input_grad,
        grad_query,
        grad_key,
        grad_value,
        grad_out_proj,
        gain_shares[0],
        gain_shares[1],
        gain_shares[2],
        gain_shares[3],
        grad_gate,
        grad_up,
        grad_down,
    )


BLOCK = 256
HALF = HD // 2
QUARTER = HD // 4
NT = (((1,), (1,)), ((), ()))
TN = (((0,), (0,)), ((), ()))
F32 = jnp.float32
BF16 = jnp.bfloat16


def dot(a, b, dims=(((1,), (0,)), ((), ()))):
    return lax.dot_general(a, b, dims, preferred_element_type=F32)


def turn(x, cosine, sine):
    return x * cosine + pltpu.roll(x, QUARTER, 1) * sine


def qkv_kernel(x_ref, gain_ref, w_ref, tab_ref, normed_ref, q_ref, kv_ref):
    core = lax.rem(lax.axis_index("shard"), 2)
    x = x_ref[...].astype(F32)
    normed = (x * inv_rms(x) * gain_ref[...]).astype(BF16)
    normed_ref[...] = normed
    lin = dot(normed, w_ref[...])
    tab = tab_ref[...]
    c0, s0, c1, s1 = (tab[:, i * HALF : (i + 1) * HALF] for i in range(4))
    scale = HD ** (-0.5)
    q_ref[:, :HALF] = (turn(lin[:, :HALF], c0, s0) * scale).astype(BF16)
    q_ref[:, HALF:] = (turn(lin[:, HALF:HD], c1, s1) * scale).astype(BF16)
    first = core == 0
    ck = jnp.where(first, c0, c1)
    sk = jnp.where(first, s0, s1)
    kv_ref[:, :HALF] = turn(lin[:, HD : HD + HALF], ck, sk).astype(BF16)
    kv_ref[:, HALF:] = lin[:, HD + HALF :].astype(BF16)


def visible_block(low_row, i, j):
    key = j * BLOCK + lax.broadcasted_iota(jnp.int32, (BLOCK, BLOCK), 0)
    query = i * BLOCK + lax.broadcasted_iota(jnp.int32, (BLOCK, BLOCK), 1)
    return (key <= query) & (key >= low_row)


def block_ranges(i):
    whole = PROMPT // BLOCK
    full = jnp.minimum(i, whole)
    return full, full, i + 1


def attend_kernel(q_ref, k_ref, v_ref, low_ref, wo_ref, att_ref, lse_ref, part_ref):
    i = pl.program_id(0)
    q = q_ref[...]
    low_row = low_ref[...]

    def step(j, carry, masked):
        acc, total = carry
        rows = pl.ds(pl.multiple_of(j * BLOCK, BLOCK), BLOCK)
        s = dot(k_ref[rows, :], q, NT)
        p = jnp.exp(CAP * jnp.tanh(s * (1.0 / CAP)))
        if masked:
            p = jnp.where(visible_block(low_row, i, j), p, 0.0)
        total = total + jnp.sum(p, axis=0, keepdims=True)
        acc = acc + dot(v_ref[rows, :], p.astype(BF16), TN)
        return acc, total

    full, start, stop = block_ranges(i)
    carry = (jnp.zeros((HD, BLOCK), F32), jnp.zeros((1, BLOCK), F32))
    carry = lax.fori_loop(0, full, functools.partial(step, masked=False), carry)
    acc, total = lax.fori_loop(start, stop, functools.partial(step, masked=True), carry)
    lse_ref[...] = jnp.log(total)
    att = (acc / total).T.astype(BF16)
    att_ref[...] = att
    part_ref[...] = dot(att, wo_ref[...]).astype(BF16)


def attend_back_kernel(
    q_ref, k_ref, v_ref, low_ref, lse_ref, att_ref, g_ref, wo_ref, tab_ref,
    dq_ref, dk_ref, dv_ref, go_ref, dk_acc, dv_acc, go_acc,
):
    i = pl.program_id(0)

    @pl.when(i == 0)
    def _():
        dk_acc[...] = jnp.zeros_like(dk_acc)
        dv_acc[...] = jnp.zeros_like(dv_acc)
        go_acc[...] = jnp.zeros_like(go_acc)

    q = q_ref[...]
    g = g_ref[...]
    att = att_ref[...]
    low_row = low_ref[...]
    lse_row = lse_ref[...]
    go_acc[...] += dot(att, g, TN)
    da = dot(g, wo_ref[...], NT).astype(BF16)
    weighted = da.astype(F32) * att.astype(F32)
    d_row = jnp.sum(weighted.T, axis=0, keepdims=True)

    def step(j, dq, masked):
        rows = pl.ds(pl.multiple_of(j * BLOCK, BLOCK), BLOCK)
        k = k_ref[rows, :]
        bent = jnp.tanh(dot(k, q, NT) * (1.0 / CAP))
        p = jnp.exp(CAP * bent - lse_row)
        if masked:
            p = jnp.where(visible_block(low_row, i, j), p, 0.0)
        dp = dot(v_ref[rows, :], da, NT)
        ds = (p * (dp - d_row) * (1.0 - bent * bent)).astype(BF16)
        dk_acc[rows, :] += dot(ds, q)
        dv_acc[rows, :] += dot(p.astype(BF16), da)
        return dq + dot(ds, k, TN)

    full, start, stop = block_ranges(i)
    dq = jnp.zeros((BLOCK, HD), F32)
    dq = lax.fori_loop(0, full, functools.partial(step, masked=False), dq)
    dq = lax.fori_loop(start, stop, functools.partial(step, masked=True), dq)
    dq = dq * HD ** (-0.5)
    tab = tab_ref[...]
    c0, s0, c1, s1 = (tab[:, n * HALF : (n + 1) * HALF] for n in range(4))
    dq_ref[:, :HALF] = turn(dq[:, :HALF], c0, -s0).astype(BF16)
    dq_ref[:, HALF:] = turn(dq[:, HALF:], c1, -s1).astype(BF16)

    @pl.when(i == pl.num_programs(0) - 1)
    def _():
        dk_ref[...] = dk_acc[...].astype(BF16)
        dv_ref[...] = dv_acc[...].astype(BF16)
        go_ref[...] = go_acc[...].astype(BF16)


def rows_spec(cols):
    return pl.BlockSpec((BLOCK, cols), lambda i: (i, 0))


def whole_spec(rows, cols):
    return pl.BlockSpec((rows, cols), lambda i: (0, 0))


def lane_spec():
    return pl.BlockSpec((1, BLOCK), lambda i: (0, i))


def kernel_params():
    return pltpu.CompilerParams(
        dimension_semantics=("arbitrary",), vmem_limit_bytes=48 * 1024 * 1024
    )


def qkv_call(x, gain, weights, table):
    rows, width = x.shape
    cols = weights.shape[1]
    return pl.pallas_call(
        qkv_kernel,
        grid=(rows // BLOCK,),
        in_specs=[rows_spec(width), whole_spec(1, width), whole_spec(width, cols), rows_spec(cols)],
        out_specs=[rows_spec(width), rows_spec(HD), rows_spec(HD)],
        out_shape=[
            jax.ShapeDtypeStruct((rows, width), BF16),
            jax.ShapeDtypeStruct((rows, HD), BF16),
            jax.ShapeDtypeStruct((rows, HD), BF16),
        ],
        compiler_params=kernel_params(),
        cost_estimate=pl.CostEstimate(
            flops=2 * rows * width * cols, bytes_accessed=4 * rows * width, transcendentals=0
        ),
        name="qkv",
    )(x, gain, weights, table)


def attend_call(q, k, v, low_row, wo):
    rows = q.shape[0]
    width = wo.shape[1]
    return pl.pallas_call(
        attend_kernel,
        grid=(rows // BLOCK,),
        in_specs=[
            rows_spec(HD), whole_spec(rows, HD), whole_spec(rows, HD), lane_spec(),
            whole_spec(HD, width),
        ],
        out_specs=[rows_spec(HD), lane_spec(), rows_spec(width)],
        out_shape=[
            jax.ShapeDtypeStruct((rows, HD), BF16),
            jax.ShapeDtypeStruct((1, rows), F32),
            jax.ShapeDtypeStruct((rows, width), BF16),
        ],
        compiler_params=kernel_params(),
        cost_estimate=pl.CostEstimate(
            flops=3 * rows * rows * HD + 2 * rows * width * HD,
            bytes_accessed=2 * rows * width,
            transcendentals=rows * rows,
        ),
        name="attend",
    )(q, k, v, low_row, wo)


def attend_back_call(q, k, v, low_row, lse, att, g, wo, table):
    rows = q.shape[0]
    width = wo.shape[1]
    return pl.pallas_call(
        attend_back_kernel,
        grid=(rows // BLOCK,),
        in_specs=[
            rows_spec(HD), whole_spec(rows, HD), whole_spec(rows, HD), lane_spec(), lane_spec(),
            rows_spec(HD), rows_spec(width), whole_spec(HD, width), rows_spec(4 * HALF),
        ],
        out_specs=[
            rows_spec(HD), whole_spec(rows, HD), whole_spec(rows, HD), whole_spec(HD, width),
        ],
        out_shape=[
            jax.ShapeDtypeStruct((rows, HD), BF16),
            jax.ShapeDtypeStruct((rows, HD), BF16),
            jax.ShapeDtypeStruct((rows, HD), BF16),
            jax.ShapeDtypeStruct((HD, width), BF16),
        ],
        scratch_shapes=[
            pltpu.VMEM((rows, HD), F32),
            pltpu.VMEM((rows, HD), F32),
            pltpu.VMEM((HD, width), F32),
        ],
        compiler_params=kernel_params(),
        cost_estimate=pl.CostEstimate(
            flops=6 * rows * rows * HD + 4 * rows * width * HD,
            bytes_accessed=2 * rows * width,
            transcendentals=rows * rows,
        ),
        name="attend_back",
    )(q, k, v, low_row, lse, att, g, wo, table)


def swap_cores(x):
    n = lax.axis_size("shard")
    return lax.ppermute(x, "shard", [(s, s ^ 1) for s in range(n)])


def gather(x, axis_name, axis):
    return lax.all_gather(x, axis_name, axis=axis, tiled=True)


def scatter(x, axis_name, axis):
    return lax.psum_scatter(x, axis_name, scatter_dimension=axis, tiled=True)


def partner(x, bit, after=None):
    n = lax.axis_size("replica")
    got = lax.ppermute(x, "replica", [(r, r ^ bit) for r in range(n)])
    return got if after is None else lax.optimization_barrier((got, after))[0]


def halve(x, axis, bit, after=None):
    half = x.shape[axis] // 2
    mine = lax.rem(lax.axis_index("replica") // bit, 2)
    kept = lax.dynamic_slice_in_dim(x, mine * half, half, axis)
    sent = lax.dynamic_slice_in_dim(x, (1 - mine) * half, half, axis)
    return (kept.astype(F32) + partner(sent, bit, after).astype(F32)).astype(BF16)


def double(x, axis, bit, after=None):
    other = partner(x, bit, after)
    mine = lax.rem(lax.axis_index("replica") // bit, 2) == 0
    return jnp.concatenate(
        [jnp.where(mine, x, other), jnp.where(mine, other, x)], axis=axis
    )


def sum_replicas(x, after=(None, None, None, None)):
    half = x.shape[0] // 2
    parts = []
    for piece, first, second in ((x[:half], 1, 2), (x[half:], 2, 1)):
        piece = halve(halve(piece, 0, first, after[0]), 0, second, after[1])
        parts.append(double(double(piece, 0, second, after[2]), 0, first, after[3]))
    return jnp.concatenate(parts).astype(F32)


def exchange(x):
    return lax.all_to_all(x, "shard", 0, 0, tiled=True)


def fast_on_device(
    tokens,
    w_query,
    w_key,
    w_value,
    w_output,
    gain_attn_in,
    gain_attn_out,
    gain_ffn_in,
    gain_ffn_out,
    w_gate,
    w_up,
    w_down,
    segment_ids,
    cotangent,
):
    tok_rows, width = tokens.shape
    w_rows = w_query.shape[0]
    shards = lax.axis_size("shard")
    replicas = lax.axis_size("replica")
    group_rows = tok_rows * shards
    shard_index = lax.axis_index("shard")
    first_core = lax.rem(shard_index, 2) == 0
    piece = w_rows // replicas

    x_group = gather(tokens, "shard", 0)
    gain_stack = jnp.stack([gain_attn_in, gain_attn_out, gain_ffn_in, gain_ffn_out])
    gains = gather(gain_stack, "shard", 1).astype(F32)

    start = lax.axis_index("replica") * piece
    wq = lax.dynamic_slice_in_dim(w_query, start, piece)
    wk = lax.dynamic_slice_in_dim(w_key, start, piece)
    wv = lax.dynamic_slice_in_dim(w_value, start, piece)
    sent = jnp.concatenate(
        [
            wq.reshape(piece, H, 2, 2, QUARTER).swapaxes(2, 3).reshape(piece, H, HD),
            wk.reshape(piece, KV, 2, 2, QUARTER).swapaxes(2, 3).reshape(piece, H, HALF),
            wv.reshape(piece, H, HALF),
        ],
        axis=2,
    ).swapaxes(0, 1)
    head_w = gather(exchange(sent), "replica", 1).reshape(width, 2 * HD)

    segment_row = segment_ids[0]
    smaller = jnp.sum((segment_row[:, None] < segment_row[None, :]).astype(jnp.int32), axis=0)
    earlier = jnp.concatenate([jnp.zeros((PROMPT,), jnp.int32), PROMPT + smaller])
    index = jnp.arange(group_rows, dtype=jnp.int32)
    low_row = earlier[None, :]
    positions = jnp.where(index < PROMPT, index, index - (earlier - PROMPT))
    rates = THETA ** (-(jnp.arange(HALF, dtype=F32) * 2.0) / HD)
    angles = positions.astype(F32)[:, None] * rates[None, :]
    cosine = jnp.cos(angles)
    sine = jnp.sin(angles)
    table = jnp.concatenate(
        [
            cosine[:, :QUARTER], cosine[:, :QUARTER], -sine[:, :QUARTER], sine[:, :QUARTER],
            cosine[:, QUARTER:], cosine[:, QUARTER:], -sine[:, QUARTER:], sine[:, QUARTER:],
        ],
        axis=1,
    )

    normed, queries, kv_own = qkv_call(x_group, gains[0:1], head_w, table)
    kv_other = swap_cores(kv_own)
    kv_low = jnp.where(first_core, kv_own, kv_other)
    kv_high = jnp.where(first_core, kv_other, kv_own)
    keys = jnp.concatenate([kv_low[:, :HALF], kv_high[:, :HALF]], axis=1)
    values = jnp.concatenate([kv_low[:, HALF:], kv_high[:, HALF:]], axis=1)
    attended, lse, raw_part = attend_call(queries, keys, values, low_row, w_output)
    raw_attn = scatter(raw_part, "shard", 0).astype(F32)

    x_float = tokens.astype(F32)
    grad_top = cotangent.astype(F32)
    chunks = 2
    size = tok_rows // chunks

    hidden_parts, normed_groups, raw_parts = [], [], []
    glus, gates, ups = [], [], []
    for c in range(chunks):
        rows = slice(c * size, (c + 1) * size)
        hidden = x_float[rows] + rms_scaled(raw_attn[rows], gains[1])
        hidden_parts.append(hidden)
        normed_groups.append(gather(rms_scaled(hidden, gains[2]).astype(BF16), "shard", 0))
    for c in range(chunks):
        gate = jnp.einsum("td,fd->tf", normed_groups[c], w_gate, preferred_element_type=F32)
        up = jnp.einsum("td,fd->tf", normed_groups[c], w_up, preferred_element_type=F32)
        glu = glu_value(gate, up).astype(BF16)
        gates.append(gate)
        ups.append(up)
        glus.append(glu)
        raw_parts.append(scatter(dot(glu, w_down).astype(BF16), "shard", 0).astype(F32))
    outs, d_groups, gain_four = [], [], []
    for c in range(chunks):
        rows = slice(c * size, (c + 1) * size)
        outs.append((hidden_parts[c] + rms_scaled(raw_parts[c], gains[3])).astype(BF16))
        _, pull = jax.vjp(rms_scaled, raw_parts[c], gains[3])
        d_raw, g4 = pull(grad_top[rows])
        gain_four.append(g4)
        d_groups.append(gather(d_raw.astype(BF16), "shard", 0))
    d_normed_parts, d_gates, d_ups = [], [], []
    for c in range(chunks):
        d_glu = jnp.einsum("td,fd->tf", d_groups[c], w_down, preferred_element_type=F32)
        _, pull = jax.vjp(glu_value, gates[c], ups[c])
        d_gate, d_up = pull(d_glu)
        d_gate, d_up = d_gate.astype(BF16), d_up.astype(BF16)
        d_gates.append(d_gate)
        d_ups.append(d_up)
        part = (dot(d_gate, w_gate) + dot(d_up, w_up)).astype(BF16)
        d_normed_parts.append(scatter(part, "shard", 0).astype(F32))

    def over_tokens(left, right):
        total = dot(left[0], right[0], TN)
        for c in range(1, chunks):
            total = total + dot(left[c], right[c], TN)
        return total.astype(BF16)

    sum_down = over_tokens(glus, d_groups)
    sum_gate = over_tokens(d_gates, normed_groups)
    sum_up = over_tokens(d_ups, normed_groups)
    d_normed_parts[-1] = lax.optimization_barrier(
        (d_normed_parts[-1], sum_down, sum_gate, sum_up)
    )[0]

    d_hiddens, d_raws, gain_two, gain_three = [], [], [], []
    for c in range(chunks):
        rows = slice(c * size, (c + 1) * size)
        _, pull = jax.vjp(rms_scaled, hidden_parts[c], gains[2])
        part, g3 = pull(d_normed_parts[c])
        d_hidden = grad_top[rows] + part
        _, pull = jax.vjp(rms_scaled, raw_attn[rows], gains[1])
        d_raw, g2 = pull(d_hidden)
        gain_two.append(g2)
        gain_three.append(g3)
        d_hiddens.append(d_hidden)
        d_raws.append(d_raw.astype(BF16))
    d_hidden = jnp.concatenate(d_hiddens)
    d_raw_low = jnp.concatenate(d_raws)
    d_raw_group = gather(d_raw_low, "shard", 0)

    dq, dk, dv, grad_out = attend_back_call(
        queries, keys, values, low_row, lse, attended, d_raw_group, w_output, table
    )
    grad_down = sum_replicas(sum_down, (d_raw_low, None, None, dq))
    grad_gate = sum_replicas(sum_gate, (d_raw_low, None, None, dq))
    grad_up = sum_replicas(sum_up, (d_raw_low, dq, None, None))
    dkv_low = jnp.concatenate([dk[:, :HALF], dv[:, :HALF]], axis=1)
    dkv_high = jnp.concatenate([dk[:, HALF:], dv[:, HALF:]], axis=1)
    dkv_mine = jnp.where(first_core, dkv_low, dkv_high).astype(F32)
    dkv = dkv_mine + swap_cores(jnp.where(first_core, dkv_high, dkv_low)).astype(F32)
    dk_half = dkv[:, :HALF]
    own = jnp.where(first_core, table[:, :HD], table[:, HD:])
    turned = jnp.concatenate([dk_half[:, QUARTER:], dk_half[:, :QUARTER]], axis=1)
    dk_lin = dk_half * own[:, :HALF] - turned * own[:, HALF:]
    d_lin = jnp.concatenate([dq, dk_lin.astype(BF16), dkv[:, HALF:].astype(BF16)], axis=1)
    part, d_lin = lax.optimization_barrier((dot(d_lin, head_w, NT).astype(BF16), d_lin))
    d_normed = scatter(part, "shard", 0).astype(F32)
    grad_head = dot(normed, d_lin, TN)
    gain_one = jnp.sum(grad_head * head_w.astype(F32), axis=1) / gains[0]
    _, pull = jax.vjp(rms_scaled, x_float, gains[0])
    input_grad = d_hidden + pull(d_normed)[0]

    gain_terms = jnp.stack([gain_one, sum(gain_two), sum(gain_three), sum(gain_four)], axis=1)
    padded = jnp.pad(gain_terms, ((0, 0), (0, HALF - gain_terms.shape[1])))
    moved = jnp.concatenate([grad_head, padded], axis=1).astype(BF16)
    moved = moved.reshape(shards, w_rows, moved.shape[1])
    cut = HD + HALF
    left = halve(halve(moved[:, :, :cut], 1, 1), 1, 2)
    right = halve(halve(moved[:, :, cut:], 1, 2), 1, 1)
    traded = exchange(jnp.concatenate([left, right], axis=2))
    left = double(double(traded[:, :, :cut], 1, 2), 1, 1).astype(F32)
    right = double(double(traded[:, :, cut:], 1, 1), 1, 2).astype(F32)
    grad_query = (
        left[:, :, :HD].reshape(H, w_rows, 2, 2, QUARTER).transpose(1, 0, 3, 2, 4)
    ).reshape(w_rows, H * HD)
    grad_key = (
        left[:, :, HD:]
        .reshape(KV, 2, w_rows, 2, QUARTER)
        .transpose(2, 0, 3, 1, 4)
        .reshape(w_rows, KV * HD)
    )
    grad_value = right[:, :, :HALF].transpose(1, 0, 2).reshape(w_rows, KV * HD)
    grad_out_proj = sum_replicas(grad_out)
    gain_shares = jnp.sum(right[:, :, HALF : HALF + gain_terms.shape[1]], axis=0).T
    return (
        jnp.concatenate(outs),
        input_grad,
        grad_query,
        grad_key,
        grad_value,
        grad_out_proj,
        gain_shares[0],
        gain_shares[1],
        gain_shares[2],
        gain_shares[3],
        grad_gate,
        grad_up,
        grad_down,
    )


def solution(mesh):
    placed = (
        P(("replica", "shard"), None),
        P("shard", None),
        P("shard", None),
        P("shard", None),
        P("shard", None),
        P("shard"),
        P("shard"),
        P("shard"),
        P("shard"),
        P("shard", None),
        P("shard", None),
        P("shard", None),
        P("replica", None),
        P(("replica", "shard"), None),
    )
    heads_fit = mesh.shape["shard"] == H and H == 2 * KV and mesh.shape["replica"] == 4
    body = fast_on_device if heads_fit else on_device
    return jax.shard_map(
        body,
        mesh=mesh,
        in_specs=placed,
        out_specs=(
            P(("replica", "shard"), None),
            P(("replica", "shard"), None),
            P("shard", None),
            P("shard", None),
            P("shard", None),
            P("shard", None),
            P("shard"),
            P("shard"),
            P("shard"),
            P("shard"),
            P("shard", None),
            P("shard", None),
            P("shard", None),
        ),
        check_vma=False,
    )
```

```python
import functools

import jax
import jax.numpy as jnp
from jax import lax
from jax.experimental import pallas as pl
from jax.experimental.pallas import tpu as pltpu
from jax.sharding import PartitionSpec as P

H = 8
KV = 4
HD = 256
PROMPT = 1024


EPS = 1e-06
CAP = 50.0
THETA = 10000.0
NEGATIVE = -1e30


def inv_rms(values):
    return lax.rsqrt(jnp.mean(values * values, axis=-1, keepdims=True) + EPS)


def rms_scaled(values, gain):
    return values * inv_rms(values) * gain


def rotate(values, positions, head_count, head_dim, sign):
    tok_count = values.shape[0]
    half = head_dim // 2
    rates = THETA ** (-(jnp.arange(half, dtype=jnp.float32) * 2.0) / head_dim)
    angles = positions.astype(jnp.float32)[:, None] * rates[None, :]
    cosine = jnp.cos(angles)[:, None, :]
    sine = sign * jnp.sin(angles)[:, None, :]
    shaped = values.reshape(tok_count, head_count, head_dim)
    first = shaped[:, :, :half]
    second = shaped[:, :, half:]
    turned = jnp.concatenate(
        [first * cosine - second * sine, second * cosine + first * sine], axis=-1
    )
    return turned.reshape(tok_count, head_count * head_dim)


def glu_value(gate, up):
    return jax.nn.gelu(gate, approximate=True) * up


def on_device(
    tokens,
    w_query,
    w_key,
    w_value,
    w_output,
    gain_attn_in,
    gain_attn_out,
    gain_ffn_in,
    gain_ffn_out,
    w_gate,
    w_up,
    w_down,
    segment_ids,
    cotangent,
):
    tok_rows = tokens.shape[0]
    query_cols = w_query.shape[1]
    kv_cols = w_key.shape[1]
    group_rows = tok_rows * lax.axis_size("shard")
    head_group = H // KV
    shard_index = lax.axis_index("shard")
    start_row = shard_index * tok_rows
    segment_row = segment_ids[0]
    key_segments = jnp.concatenate([jnp.full((PROMPT,), -1, jnp.int32), segment_row])
    key_index = jnp.arange(group_rows, dtype=jnp.int32)
    query_index = start_row + jnp.arange(tok_rows, dtype=jnp.int32)
    query_segments = lax.dynamic_slice_in_dim(key_segments, start_row, tok_rows)
    earlier = jnp.sum((segment_row[None, :] < query_segments[:, None]).astype(jnp.int32), axis=1)
    positions = query_index - earlier
    visible = (key_index[None, :] <= query_index[:, None]) & (
        (key_index[None, :] < PROMPT) | (key_segments[None, :] == query_segments[:, None])
    )
    gain_stack = jnp.stack([gain_attn_in, gain_attn_out, gain_ffn_in, gain_ffn_out])
    full_query, full_key, full_value, full_out, gains = (
        lax.all_gather(w_query, "shard", axis=0, tiled=True),
        lax.all_gather(w_key, "shard", axis=0, tiled=True),
        lax.all_gather(w_value, "shard", axis=0, tiled=True),
        lax.all_gather(w_output, "shard", axis=0, tiled=True),
        lax.all_gather(gain_stack, "shard", axis=1, tiled=True),
    )
    gain_first = gains[0].astype(jnp.float32)
    gain_second = gains[1].astype(jnp.float32)
    gain_third = gains[2].astype(jnp.float32)
    gain_fourth = gains[3].astype(jnp.float32)
    x_float = tokens.astype(jnp.float32)
    normed = rms_scaled(x_float, gain_first).astype(jnp.bfloat16)
    query_lin = jnp.dot(normed, full_query, preferred_element_type=jnp.float32)
    key_lin = jnp.dot(normed, full_key, preferred_element_type=jnp.float32)
    value_lin = jnp.dot(normed, full_value, preferred_element_type=jnp.float32)
    query_scale = HD ** (-0.5)
    queries = (rotate(query_lin, positions, H, HD, 1.0) * query_scale).astype(jnp.bfloat16)
    keys = rotate(key_lin, positions, KV, HD, 1.0).astype(jnp.bfloat16)
    values = value_lin.astype(jnp.bfloat16)
    group_keys, group_values = (
        lax.all_gather(keys, "shard", axis=0, tiled=True),
        lax.all_gather(values, "shard", axis=0, tiled=True),
    )
    keys_shaped = group_keys.reshape(group_rows, KV, HD)
    values_shaped = group_values.reshape(group_rows, KV, HD)
    query_shaped = queries.reshape(tok_rows, KV, head_group, HD)

    def capped_scores():
        scores = jnp.einsum(
            "qkgd,pkd->kgqp", query_shaped, keys_shaped, preferred_element_type=jnp.float32
        )
        bent = jnp.tanh(scores / CAP)
        return (bent, jnp.where(visible[None, None], CAP * bent, NEGATIVE))

    bent, capped = capped_scores()
    highest = jnp.max(capped, axis=-1, keepdims=True)
    log_total = highest + jnp.log(jnp.sum(jnp.exp(capped - highest), axis=-1, keepdims=True))
    probs = jnp.exp(capped - log_total)
    probs_low = probs.astype(jnp.bfloat16)
    attended = jnp.einsum(
        "kgqp,pkd->qkgd", probs_low, values_shaped, preferred_element_type=jnp.float32
    )
    attended_low = attended.reshape(tok_rows, query_cols).astype(jnp.bfloat16)
    raw_attn = jnp.dot(attended_low, full_out, preferred_element_type=jnp.float32)
    hidden_state = x_float + rms_scaled(raw_attn, gain_second)
    normed_ffn = rms_scaled(hidden_state, gain_third).astype(jnp.bfloat16)
    group_normed = lax.all_gather(normed_ffn, "shard", axis=0, tiled=True)
    gate = jnp.einsum("td,fd->tf", group_normed, w_gate, preferred_element_type=jnp.float32)
    up = jnp.einsum("td,fd->tf", group_normed, w_up, preferred_element_type=jnp.float32)
    glu = glu_value(gate, up).astype(jnp.bfloat16)
    raw_ffn = lax.psum_scatter(
        jnp.dot(glu, w_down, preferred_element_type=jnp.float32).astype(jnp.bfloat16),
        "shard",
        scatter_dimension=0,
        tiled=True,
    ).astype(jnp.float32)
    output = (hidden_state + rms_scaled(raw_ffn, gain_fourth)).astype(jnp.bfloat16)
    grad_top = cotangent.astype(jnp.float32)
    _, pull_fourth = jax.vjp(rms_scaled, raw_ffn, gain_fourth)
    d_raw_ffn, grad_gain_fourth = pull_fourth(grad_top)
    d_raw_low = d_raw_ffn.astype(jnp.bfloat16)
    group_d_raw = lax.all_gather(d_raw_low, "shard", axis=0, tiled=True)
    grad_down = jnp.einsum("tf,td->fd", glu, group_d_raw, preferred_element_type=jnp.float32)
    d_glu = jnp.einsum("td,fd->tf", group_d_raw, w_down, preferred_element_type=jnp.float32)
    _, pull_glu = jax.vjp(glu_value, gate, up)
    d_gate, d_up = pull_glu(d_glu)
    d_gate_low = d_gate.astype(jnp.bfloat16)
    d_up_low = d_up.astype(jnp.bfloat16)
    grad_gate = jnp.einsum(
        "tf,td->fd", d_gate_low, group_normed, preferred_element_type=jnp.float32
    )
    grad_up = jnp.einsum("tf,td->fd", d_up_low, group_normed, preferred_element_type=jnp.float32)
    gate_part = jnp.dot(d_gate_low, w_gate, preferred_element_type=jnp.float32)
    up_part = jnp.dot(d_up_low, w_up, preferred_element_type=jnp.float32)
    d_normed_ffn = lax.psum_scatter(
        (gate_part + up_part).astype(jnp.bfloat16), "shard", scatter_dimension=0, tiled=True
    ).astype(jnp.float32)
    _, pull_third = jax.vjp(rms_scaled, hidden_state, gain_third)
    d_hidden_part, grad_gain_third = pull_third(d_normed_ffn)
    d_hidden = grad_top + d_hidden_part
    _, pull_second = jax.vjp(rms_scaled, raw_attn, gain_second)
    d_raw_attn, grad_gain_second = pull_second(d_hidden)
    d_raw_attn_low = d_raw_attn.astype(jnp.bfloat16)
    picked = attended_low
    grad_out_proj = lax.psum_scatter(
        jnp.einsum("tf,td->fd", picked, d_raw_attn_low, preferred_element_type=jnp.float32).astype(
            jnp.bfloat16
        ),
        "shard",
        scatter_dimension=0,
        tiled=True,
    ).astype(jnp.float32)
    d_attended_low = jnp.einsum(
        "td,fd->tf", d_raw_attn_low, full_out, preferred_element_type=jnp.float32
    ).astype(jnp.bfloat16)
    d_attended_shaped = d_attended_low.reshape(tok_rows, KV, head_group, HD)
    bent_again, capped_again = capped_scores()
    probs_again = jnp.exp(capped_again - log_total)
    probs_again_low = probs_again.astype(jnp.bfloat16)
    d_probs = jnp.einsum(
        "qkgd,pkd->kgqp", d_attended_shaped, values_shaped, preferred_element_type=jnp.float32
    )
    d_capped = probs_again * (d_probs - jnp.sum(probs_again * d_probs, axis=-1, keepdims=True))
    d_scores_low = (d_capped * (1.0 - bent_again * bent_again)).astype(jnp.bfloat16)
    d_queries = jnp.einsum(
        "kgqp,pkd->qkgd", d_scores_low, keys_shaped, preferred_element_type=jnp.float32
    ).reshape(tok_rows, query_cols)
    d_keys_group = jnp.einsum(
        "kgqp,qkgd->pkd", d_scores_low, query_shaped, preferred_element_type=jnp.float32
    ).reshape(group_rows, kv_cols)
    d_values_group = jnp.einsum(
        "kgqp,qkgd->pkd", probs_again_low, d_attended_shaped, preferred_element_type=jnp.float32
    ).reshape(group_rows, kv_cols)
    d_keys, d_values = (
        lax.psum_scatter(
            d_keys_group.astype(jnp.bfloat16), "shard", scatter_dimension=0, tiled=True
        ).astype(jnp.float32),
        lax.psum_scatter(
            d_values_group.astype(jnp.bfloat16), "shard", scatter_dimension=0, tiled=True
        ).astype(jnp.float32),
    )
    d_query_low = rotate(d_queries * query_scale, positions, H, HD, -1.0).astype(jnp.bfloat16)
    d_key_low = rotate(d_keys, positions, KV, HD, -1.0).astype(jnp.bfloat16)
    d_value_low = d_values.astype(jnp.bfloat16)
    d_normed = jnp.einsum("tf,df->td", d_query_low, full_query, preferred_element_type=jnp.float32)
    d_normed = d_normed + jnp.einsum(
        "tf,df->td", d_key_low, full_key, preferred_element_type=jnp.float32
    )
    d_normed = d_normed + jnp.einsum(
        "tf,df->td", d_value_low, full_value, preferred_element_type=jnp.float32
    )
    _, pull_first = jax.vjp(rms_scaled, x_float, gain_first)
    d_input_part, grad_gain_first = pull_first(d_normed)
    input_grad = d_hidden + d_input_part
    d_projected = jnp.concatenate([d_query_low, d_key_low, d_value_low], axis=1)
    picked = normed
    grad_projected = lax.psum_scatter(
        jnp.einsum("tc,tf->cf", picked, d_projected, preferred_element_type=jnp.float32).astype(
            jnp.bfloat16
        ),
        "shard",
        scatter_dimension=0,
        tiled=True,
    ).astype(jnp.float32)
    grad_query = grad_projected[:, :query_cols]
    grad_key = grad_projected[:, query_cols : query_cols + kv_cols]
    grad_value = grad_projected[:, query_cols + kv_cols :]
    gain_terms = jnp.stack([grad_gain_first, grad_gain_second, grad_gain_third, grad_gain_fourth])
    gain_shares = lax.psum_scatter(
        gain_terms.astype(jnp.bfloat16), "shard", scatter_dimension=1, tiled=True
    ).astype(jnp.float32)
    grad_query, grad_key, grad_value, grad_out_proj, gain_shares, grad_gate, grad_up, grad_down = (
        lax.psum(grad_query.astype(jnp.bfloat16), "replica").astype(jnp.float32),
        lax.psum(grad_key.astype(jnp.bfloat16), "replica").astype(jnp.float32),
        lax.psum(grad_value.astype(jnp.bfloat16), "replica").astype(jnp.float32),
        lax.psum(grad_out_proj.astype(jnp.bfloat16), "replica").astype(jnp.float32),
        lax.psum(gain_shares.astype(jnp.bfloat16), "replica").astype(jnp.float32),
        lax.psum(grad_gate.astype(jnp.bfloat16), "replica").astype(jnp.float32),
        lax.psum(grad_up.astype(jnp.bfloat16), "replica").astype(jnp.float32),
        lax.psum(grad_down.astype(jnp.bfloat16), "replica").astype(jnp.float32),
    )
    return (
        output,
        input_grad,
        grad_query,
        grad_key,
        grad_value,
        grad_out_proj,
        gain_shares[0],
        gain_shares[1],
        gain_shares[2],
        gain_shares[3],
        grad_gate,
        grad_up,
        grad_down,
    )


BLOCK = 256
HALF = HD // 2
QUARTER = HD // 4
NT = (((1,), (1,)), ((), ()))
TN = (((0,), (0,)), ((), ()))
F32 = jnp.float32
BF16 = jnp.bfloat16


def dot(a, b, dims=(((1,), (0,)), ((), ()))):
    return lax.dot_general(a, b, dims, preferred_element_type=F32)


def turn(x, cosine, sine):
    return x * cosine + pltpu.roll(x, QUARTER, 1) * sine


def qkv_kernel(x_ref, gain_ref, w_ref, tab_ref, normed_ref, q_ref, kv_ref):
    core = lax.rem(lax.axis_index("shard"), 2)
    x = x_ref[...].astype(F32)
    normed = (x * inv_rms(x) * gain_ref[...]).astype(BF16)
    normed_ref[...] = normed
    lin = dot(normed, w_ref[...])
    tab = tab_ref[...]
    c0, s0, c1, s1 = (tab[:, i * HALF : (i + 1) * HALF] for i in range(4))
    scale = HD ** (-0.5)
    q_ref[:, :HALF] = (turn(lin[:, :HALF], c0, s0) * scale).astype(BF16)
    q_ref[:, HALF:] = (turn(lin[:, HALF:HD], c1, s1) * scale).astype(BF16)
    first = core == 0
    ck = jnp.where(first, c0, c1)
    sk = jnp.where(first, s0, s1)
    kv_ref[:, :HALF] = turn(lin[:, HD : HD + HALF], ck, sk).astype(BF16)
    kv_ref[:, HALF:] = lin[:, HD + HALF :].astype(BF16)


def visible_block(low_row, i, j):
    key = j * BLOCK + lax.broadcasted_iota(jnp.int32, (BLOCK, BLOCK), 0)
    query = i * BLOCK + lax.broadcasted_iota(jnp.int32, (BLOCK, BLOCK), 1)
    return (key <= query) & (key >= low_row)


def block_ranges(i):
    whole = PROMPT // BLOCK
    full = jnp.minimum(i, whole)
    return full, full, i + 1


def attend_kernel(q_ref, k_ref, v_ref, low_ref, wo_ref, att_ref, lse_ref, top_ref, end_ref):
    i = pl.program_id(0)
    q = q_ref[...]
    low_row = low_ref[...]

    def step(j, carry, masked):
        acc, total = carry
        rows = pl.ds(pl.multiple_of(j * BLOCK, BLOCK), BLOCK)
        s = dot(k_ref[rows, :], q, NT)
        p = jnp.exp(CAP * jnp.tanh(s * (1.0 / CAP)))
        if masked:
            p = jnp.where(visible_block(low_row, i, j), p, 0.0)
        total = total + jnp.sum(p, axis=0, keepdims=True)
        acc = acc + dot(v_ref[rows, :], p.astype(BF16), TN)
        return acc, total

    full, start, stop = block_ranges(i)
    carry = (jnp.zeros((HD, BLOCK), F32), jnp.zeros((1, BLOCK), F32))
    carry = lax.fori_loop(0, full, functools.partial(step, masked=False), carry)
    acc, total = lax.fori_loop(start, stop, functools.partial(step, masked=True), carry)
    lse_ref[...] = jnp.log(total)
    att = (acc / total).T.astype(BF16)
    att_ref[...] = att
    part = dot(att, wo_ref[...]).astype(BF16)
    top_ref[...] = part[: BLOCK // 2]
    end_ref[...] = part[BLOCK // 2 :]


def swap_copies(sources, targets, bits, sems):
    return [
        pltpu.make_async_remote_copy(
            src_ref=src,
            dst_ref=dst,
            send_sem=sems.at[0, n],
            recv_sem=sems.at[1, n],
            device_id={"replica": flipped(bit)},
            device_id_type=pl.DeviceIdType.MESH,
        )
        for n, (src, dst, bit) in enumerate(zip(sources, targets, bits))
    ]


def attend_back_kernel(
    bits,
    q_ref, k_ref, v_ref, low_ref, lse_ref, att_ref, top_ref, end_ref, wo_ref, tab_ref,
    swap_a, swap_b,
    dq_ref, dk_ref, dv_ref, go_ref, got_a, got_b, dk_acc, dv_acc, go_acc, swap_sem,
):
    i = pl.program_id(0)
    swaps = swap_copies((swap_a, swap_b), (got_a, got_b), bits, swap_sem)

    @pl.when(i == 0)
    def _():
        barrier = pltpu.get_barrier_semaphore()
        for bit in bits:
            pl.semaphore_signal(
                barrier,
                inc=1,
                device_id={"replica": flipped(bit)},
                device_id_type=pl.DeviceIdType.MESH,
            )
        pl.semaphore_wait(barrier, len(bits))
        for swap in swaps:
            swap.start()
        dk_acc[...] = jnp.zeros_like(dk_acc)
        dv_acc[...] = jnp.zeros_like(dv_acc)
        go_acc[...] = jnp.zeros_like(go_acc)

    q = q_ref[...]
    g = jnp.concatenate([top_ref[...], end_ref[...]])
    att = att_ref[...]
    low_row = low_ref[...]
    lse_row = lse_ref[...]
    go_acc[...] += dot(att, g, TN)
    da = dot(g, wo_ref[...], NT).astype(BF16)
    weighted = da.astype(F32) * att.astype(F32)
    d_row = jnp.sum(weighted.T, axis=0, keepdims=True)

    def step(j, dq, masked):
        rows = pl.ds(pl.multiple_of(j * BLOCK, BLOCK), BLOCK)
        k = k_ref[rows, :]
        bent = jnp.tanh(dot(k, q, NT) * (1.0 / CAP))
        p = jnp.exp(CAP * bent - lse_row)
        if masked:
            p = jnp.where(visible_block(low_row, i, j), p, 0.0)
        dp = dot(v_ref[rows, :], da, NT)
        ds = (p * (dp - d_row) * (1.0 - bent * bent)).astype(BF16)
        dk_acc[rows, :] += dot(ds, q)
        dv_acc[rows, :] += dot(p.astype(BF16), da)
        return dq + dot(ds, k, TN)

    full, start, stop = block_ranges(i)
    dq = jnp.zeros((BLOCK, HD), F32)
    dq = lax.fori_loop(0, full, functools.partial(step, masked=False), dq)
    dq = lax.fori_loop(start, stop, functools.partial(step, masked=True), dq)
    dq = dq * HD ** (-0.5)
    tab = tab_ref[...]
    c0, s0, c1, s1 = (tab[:, n * HALF : (n + 1) * HALF] for n in range(4))
    dq_ref[:, :HALF] = turn(dq[:, :HALF], c0, -s0).astype(BF16)
    dq_ref[:, HALF:] = turn(dq[:, HALF:], c1, -s1).astype(BF16)

    @pl.when(i == pl.num_programs(0) - 1)
    def _():
        dk_ref[...] = dk_acc[...].astype(BF16)
        dv_ref[...] = dv_acc[...].astype(BF16)
        go_ref[...] = go_acc[...].astype(BF16)
        for swap in swaps:
            swap.wait()


ANYWHERE = pl.BlockSpec(memory_space=pl.ANY)


def rows_spec(cols):
    return pl.BlockSpec((BLOCK, cols), lambda i: (i, 0))


def half_spec(cols):
    return pl.BlockSpec((BLOCK // 2, cols), lambda i: (i, 0))


def whole_spec(rows, cols):
    return pl.BlockSpec((rows, cols), lambda i: (0, 0))


def lane_spec():
    return pl.BlockSpec((1, BLOCK), lambda i: (0, i))


def kernel_params():
    return pltpu.CompilerParams(
        dimension_semantics=("arbitrary",), vmem_limit_bytes=48 * 1024 * 1024
    )


def qkv_call(x, gain, weights, table):
    rows, width = x.shape
    cols = weights.shape[1]
    return pl.pallas_call(
        qkv_kernel,
        grid=(rows // BLOCK,),
        in_specs=[rows_spec(width), whole_spec(1, width), whole_spec(width, cols), rows_spec(cols)],
        out_specs=[rows_spec(width), rows_spec(HD), rows_spec(HD)],
        out_shape=[
            jax.ShapeDtypeStruct((rows, width), BF16),
            jax.ShapeDtypeStruct((rows, HD), BF16),
            jax.ShapeDtypeStruct((rows, HD), BF16),
        ],
        compiler_params=kernel_params(),
        cost_estimate=pl.CostEstimate(
            flops=2 * rows * width * cols, bytes_accessed=4 * rows * width, transcendentals=0
        ),
        name="qkv",
    )(x, gain, weights, table)


def attend_call(q, k, v, low_row, wo):
    rows = q.shape[0]
    width = wo.shape[1]
    return pl.pallas_call(
        attend_kernel,
        grid=(rows // BLOCK,),
        in_specs=[
            rows_spec(HD), whole_spec(rows, HD), whole_spec(rows, HD), lane_spec(),
            whole_spec(HD, width),
        ],
        out_specs=[rows_spec(HD), lane_spec(), half_spec(width), half_spec(width)],
        out_shape=[
            jax.ShapeDtypeStruct((rows, HD), BF16),
            jax.ShapeDtypeStruct((1, rows), F32),
            jax.ShapeDtypeStruct((rows // 2, width), BF16),
            jax.ShapeDtypeStruct((rows // 2, width), BF16),
        ],
        compiler_params=kernel_params(),
        cost_estimate=pl.CostEstimate(
            flops=3 * rows * rows * HD + 2 * rows * width * HD,
            bytes_accessed=2 * rows * width,
            transcendentals=rows * rows,
        ),
        name="attend",
    )(q, k, v, low_row, wo)


def attend_back_call(number, q, k, v, low_row, lse, att, top, end, wo, table, swaps):
    rows = q.shape[0]
    width = wo.shape[1]
    bits = tuple(bit for _, bit in swaps)
    sent = [x for x, _ in swaps]
    return pl.pallas_call(
        functools.partial(attend_back_kernel, bits),
        grid=(rows // BLOCK,),
        in_specs=[
            rows_spec(HD), whole_spec(rows, HD), whole_spec(rows, HD), lane_spec(), lane_spec(),
            rows_spec(HD), half_spec(width), half_spec(width), whole_spec(HD, width),
            rows_spec(4 * HALF), ANYWHERE, ANYWHERE,
        ],
        out_specs=[
            rows_spec(HD), whole_spec(rows, HD), whole_spec(rows, HD), whole_spec(HD, width),
            ANYWHERE, ANYWHERE,
        ],
        out_shape=[
            jax.ShapeDtypeStruct((rows, HD), BF16),
            jax.ShapeDtypeStruct((rows, HD), BF16),
            jax.ShapeDtypeStruct((rows, HD), BF16),
            jax.ShapeDtypeStruct((HD, width), BF16),
        ]
        + [jax.ShapeDtypeStruct(x.shape, x.dtype) for x in sent],
        scratch_shapes=[
            pltpu.VMEM((rows, HD), F32),
            pltpu.VMEM((rows, HD), F32),
            pltpu.VMEM((HD, width), F32),
            pltpu.SemaphoreType.DMA((2, len(bits))),
        ],
        compiler_params=pltpu.CompilerParams(
            dimension_semantics=("arbitrary",),
            vmem_limit_bytes=48 * 1024 * 1024,
            collective_id=number,
            has_side_effects=True,
        ),
        cost_estimate=pl.CostEstimate(
            flops=6 * rows * rows * HD + 4 * rows * width * HD,
            bytes_accessed=2 * rows * width,
            transcendentals=rows * rows,
        ),
        name="attend_back",
    )(q, k, v, low_row, lse, att, top, end, wo, table, *sent)


def gelu_parts(v):
    k = (2.0 / jnp.pi) ** 0.5
    square = v * v
    bent = jnp.tanh(k * v * (1.0 + 0.044715 * square))
    half = 0.5 * (1.0 + bent)
    slope = half + 0.5 * v * (1.0 - bent * bent) * k * (1.0 + 3 * 0.044715 * square)
    return v * half, slope


def flipped(bit):
    r = lax.axis_index("replica")
    return r + bit * (1 - 2 * lax.rem(r // bit, 2))


def greet_neighbours(chips, bits=()):
    barrier = pltpu.get_barrier_semaphore()
    for bit in bits:
        pl.semaphore_signal(
            barrier,
            inc=1,
            device_id={"replica": flipped(bit)},
            device_id_type=pl.DeviceIdType.MESH,
        )
    me = lax.axis_index("shard")
    z, core, last = me // 2, lax.rem(me, 2), chips - 1

    def greet(chip, other):
        pl.semaphore_signal(
            barrier,
            inc=1,
            device_id={"shard": chip * 2 + other},
            device_id_type=pl.DeviceIdType.MESH,
        )

    greet(z, 1 - core)

    @pl.when(z > 0)
    def _():
        greet(z - 1, core)

    @pl.when(z < last)
    def _():
        greet(z + 1, core)

    pl.semaphore_wait(barrier, 1 + len(bits) + jnp.minimum(z, 1) + jnp.minimum(last - z, 1))


class Line:
    def __init__(self, own, buf, sems, chips):
        self.own, self.buf, self.chips = own, buf, chips
        self.right, self.left, self.side, self.got, self.got_side = sems
        me = lax.axis_index("shard")
        self.z, self.core = me // 2, lax.rem(me, 2)
        self.rows = own.shape[0]

    def place(self, chip, core):
        first = pl.multiple_of((chip * 2 + core) * self.rows, self.rows)
        return self.buf.at[pl.ds(first, self.rows)]

    def move(self, chip, src, send, got, target_chip, target_core):
        return pltpu.make_async_remote_copy(
            src_ref=src,
            dst_ref=self.place(chip, self.core),
            send_sem=send.at[chip],
            recv_sem=got.at[chip],
            device_id={"shard": target_chip * 2 + target_core},
            device_id_type=pl.DeviceIdType.MESH,
        )

    def to_right(self, chip, src):
        return self.move(chip, src, self.right, self.got, self.z + 1, self.core)

    def to_left(self, chip, src):
        return self.move(chip, src, self.left, self.got, self.z - 1, self.core)

    def to_side(self, chip, src):
        return self.move(chip, src, self.side, self.got_side, self.z, 1 - self.core)

    def start(self):
        z, last = self.z, self.chips - 1

        @pl.when(z > 0)
        def _():
            self.to_left(z, self.own).start()

        @pl.when(z < last)
        def _():
            self.to_right(z, self.own).start()

        self.to_side(z, self.own).start()

    def pass_on(self, hop):
        z, last = self.z, self.chips - 1

        @pl.when((hop > 0) & (z >= hop))
        def _():
            chip = z - hop
            block = self.place(chip, self.core)
            self.to_right(chip, block).wait_recv()

            @pl.when(z < last)
            def _():
                self.to_right(chip, block).start()

            self.to_side(chip, block).start()

        @pl.when((hop > 0) & (z + hop <= last))
        def _():
            chip = z + hop
            block = self.place(chip, self.core)
            self.to_left(chip, block).wait_recv()

            @pl.when(z > 0)
            def _():
                self.to_left(chip, block).start()

            self.to_side(chip, block).start()

    def chip_at(self, step):
        z = self.z
        near = z + 1 - 2 * lax.rem(z, 2)
        high = z // 2
        by_step = (z, near, 2 - high, 3 - 3 * high)
        chip = by_step[0]
        for n in range(1, 4):
            chip = jnp.where(step == n, by_step[n], chip)
        return chip

    def wait_side(self, chip):
        pltpu.make_async_remote_copy(
            src_ref=self.place(chip, self.core),
            dst_ref=self.place(chip, 1 - self.core),
            send_sem=self.side.at[chip],
            recv_sem=self.got_side.at[chip],
            device_id={"shard": self.z * 2 + 1 - self.core},
            device_id_type=pl.DeviceIdType.MESH,
        ).wait_recv()

    def finish(self):
        z, last = self.z, self.chips - 1

        def done(chip, carry):
            @pl.when((z < last) & (chip <= z))
            def _():
                self.to_right(chip, self.place(chip, self.core)).wait_send()

            @pl.when((z > 0) & (chip >= z))
            def _():
                self.to_left(chip, self.place(chip, self.core)).wait_send()

            self.to_side(chip, self.place(chip, self.core)).wait_send()
            return carry

        lax.fori_loop(0, self.chips, done, 0)


class Chain:
    def __init__(self, part, total, total_hbm, bufs, sems, chips):
        self.part, self.total, self.total_hbm, self.chips = part, total, total_hbm, chips
        self.mine, self.side, self.from_left, self.from_right, self.stage = bufs
        (
            self.mine_sem, self.side_send, self.side_got, self.sent, self.left_got,
            self.right_got, self.total_sem,
        ) = sems
        me = lax.axis_index("shard")
        self.z, self.core = me // 2, lax.rem(me, 2)
        self.rows = self.mine.shape[1]

    def block(self, chip, core):
        first = pl.multiple_of((chip * 2 + core) * self.rows, self.rows)
        return self.part.at[pl.ds(first, self.rows)]

    def load(self, chip):
        return pltpu.make_async_copy(
            self.block(chip, self.core), self.mine.at[chip], self.mine_sem.at[chip]
        )

    def hand(self, chip):
        return pltpu.make_async_remote_copy(
            src_ref=self.block(chip, 1 - self.core),
            dst_ref=self.side.at[chip],
            send_sem=self.side_send.at[chip],
            recv_sem=self.side_got.at[chip],
            device_id={"shard": self.z * 2 + 1 - self.core},
            device_id_type=pl.DeviceIdType.MESH,
        )

    def send(self, chip, dst, got, step):
        return pltpu.make_async_remote_copy(
            src_ref=self.stage.at[chip],
            dst_ref=dst.at[chip],
            send_sem=self.sent.at[chip],
            recv_sem=got.at[chip],
            device_id={"shard": (self.z + step) * 2 + self.core},
            device_id_type=pl.DeviceIdType.MESH,
        )

    def to_right(self, chip):
        return self.send(chip, self.from_left, self.left_got, 1)

    def to_left(self, chip):
        return self.send(chip, self.from_right, self.right_got, -1)

    def start(self):
        z, last = self.z, self.chips - 1

        def begin(n, carry):
            chip = jnp.where(z * 2 <= last, last - n, n)
            self.hand(chip).start()
            self.load(chip).start()
            return carry

        lax.fori_loop(0, self.chips, begin, 0)

    def add(self, dst, chip, others):
        size = 32

        def some(n, carry):
            rows = pl.ds(pl.multiple_of(n * size, size), size)
            value = self.mine[chip, rows, :].astype(F32) + self.side[chip, rows, :].astype(F32)
            for other in others:
                value = value + other[chip, rows, :].astype(F32)
            if dst is self.total:
                dst[rows, :] = value
            else:
                dst[chip, rows, :] = value.astype(BF16)
            return carry

        lax.fori_loop(0, self.rows // size, some, 0)

    def ready(self, chip):
        self.load(chip).wait()
        self.hand(chip).wait_recv()

    def step(self, n):
        z, last = self.z, self.chips - 1

        @pl.when((n < last) & (z <= n))
        def _():
            chip = last - n + z
            self.ready(chip)

            @pl.when(z == 0)
            def _():
                self.add(self.stage, chip, ())

            @pl.when(z > 0)
            def _():
                self.to_right(chip).wait_recv()
                self.add(self.stage, chip, (self.from_left,))

            self.to_right(chip).start()

        @pl.when((n < last) & (last - z <= n))
        def _():
            chip = n - last + z
            self.ready(chip)

            @pl.when(z == last)
            def _():
                self.add(self.stage, chip, ())

            @pl.when(z < last)
            def _():
                self.to_left(chip).wait_recv()
                self.add(self.stage, chip, (self.from_right,))

            self.to_left(chip).start()

        @pl.when(n == last)
        def _():
            self.ready(z)

            @pl.when(z == 0)
            def _():
                self.to_left(z).wait_recv()
                self.add(self.total, z, (self.from_right,))

            @pl.when(z == last)
            def _():
                self.to_right(z).wait_recv()
                self.add(self.total, z, (self.from_left,))

            @pl.when((z > 0) & (z < last))
            def _():
                self.to_left(z).wait_recv()
                self.to_right(z).wait_recv()
                self.add(self.total, z, (self.from_left, self.from_right))

            pltpu.make_async_copy(self.total, self.total_hbm, self.total_sem).start()

    def finish(self):
        z = self.z

        def done(chip, carry):
            self.hand(chip).wait_send()

            @pl.when(chip != z)
            def _():
                self.to_right(chip).wait_send()

            return carry

        lax.fori_loop(0, self.chips, done, 0)
        pltpu.make_async_copy(self.total, self.total_hbm, self.total_sem).wait()


FF_TILE = 384


def forward_tiles(rows, buf, weights, ins, outs, acc, part):
    wg, wu, wd = weights
    gate, up, glu = outs
    tiles = wg.shape[0] // FF_TILE
    for t in range(tiles):
        cols = slice(t * FF_TILE, (t + 1) * FF_TILE)
        g = dot(buf[rows, :], wg[cols, :], NT)
        u = dot(buf[rows, :], wu[cols, :], NT)
        act = (gelu_parts(g)[0] * u).astype(BF16)
        gate[rows, cols] = g.astype(BF16)
        up[rows, cols] = u.astype(BF16)
        glu[rows, cols] = act
        more = dot(act, wd[cols, :])
        add_tile(t, tiles, rows, more, acc, part)


def backward_tiles(rows, buf, weights, ins, outs, acc, part):
    wg, wu, wd = weights
    gate, up = ins
    dgate, dup = outs
    tiles = wg.shape[0] // FF_TILE
    for t in range(tiles):
        cols = slice(t * FF_TILE, (t + 1) * FF_TILE)
        d_act = dot(buf[rows, :], wd[cols, :], NT)
        value, slope = gelu_parts(gate[rows, cols].astype(F32))
        dg = (d_act * up[rows, cols].astype(F32) * slope).astype(BF16)
        du = (d_act * value).astype(BF16)
        dgate[rows, cols] = dg
        dup[rows, cols] = du
        more = dot(dg, wg[cols, :]) + dot(du, wu[cols, :])
        add_tile(t, tiles, rows, more, acc, part)


def add_tile(t, tiles, rows, more, acc, part):
    if t == 0:
        acc[...] = more
    elif t < tiles - 1:
        acc[...] += more
    else:
        part[rows, :] = (acc[...] + more).astype(BF16)


def comm_kernel(tiles_of, n_saved, n_made, gathers, sums, bits, *refs):
    refs = list(refs)

    def take(n):
        out = refs[:n]
        del refs[:n]
        return out

    heavy = tiles_of is not None
    own_hbm = take(1)[0] if gathers else None
    loads_from = take(3 + n_saved) if heavy else []
    part_in = take(1)[0] if sums else None
    swap_from = take(len(bits))
    all_hbm = take(1)[0] if gathers else None
    made_hbm = take(n_made + 1) if heavy else []
    total_hbm = take(1)[0] if sums else None
    swap_to = take(len(bits))
    buf = take(1)[0] if gathers else None
    loads_to = take(3 + n_saved) if heavy else []
    made = take(n_made + 1) if heavy else []
    acc = take(1)[0] if heavy else None
    total = take(1)[0] if sums else None
    chain_bufs = take(5) if sums else None
    line_sems = take(6) if gathers else None
    chain_sems = take(7) if sums else None
    out_sem = take(1)[0] if gathers else None
    load_sem = take(1)[0] if heavy else None
    swap_sem = take(1)[0] if bits else None

    chips = lax.axis_size("shard") // 2
    greet_neighbours(chips, sorted(set(bits)))
    swaps = swap_copies(swap_from, swap_to, bits, swap_sem)
    line = chain = None
    if gathers:
        line = Line(own_hbm, buf, line_sems[:5], chips)
        line.start()
        keep = pltpu.make_async_copy(own_hbm, line.place(line.z, line.core), line_sems[5])
        keep.start()
        pair = 2 * own_hbm.shape[0]
    if sums:
        chain = Chain(part_in, total, total_hbm, chain_bufs, chain_sems, chips)
        chain.start()
    for swap in swaps:
        swap.start()
    loads = [
        pltpu.make_async_copy(src, dst, load_sem.at[n])
        for n, (src, dst) in enumerate(zip(loads_from, loads_to))
    ]
    for load in loads:
        load.start()
    if gathers:
        keep.wait()

    def outs(chip):
        rows = pl.ds(pl.multiple_of(chip * pair, pair), pair)
        return [
            pltpu.make_async_copy(src.at[rows], dst.at[rows], out_sem.at[n, chip])
            for n, (src, dst) in enumerate(zip([buf] + made, [all_hbm] + made_hbm))
        ]

    def step(n, carry):
        if gathers:
            line.pass_on(n)
        if sums and gathers:

            @pl.when(n > 0)
            def _():
                chain.step(n - 1)

        elif sums:
            chain.step(n)
        if gathers:
            chip = line.chip_at(n)
            line.wait_side(chip)
            rows = pl.ds(pl.multiple_of(chip * pair, pair), pair)
            if heavy:

                @pl.when(n == 0)
                def _():
                    for load in loads:
                        load.wait()

                tiles_of(rows, buf, loads_to[:3], loads_to[3:], made[:-1], acc, made[-1])
            for copy in outs(chip):
                copy.start()
        return carry

    lax.fori_loop(0, chips, step, 0)
    if sums and gathers:
        chain.step(chips - 1)
    if sums:
        chain.finish()
    if gathers:
        line.finish()

        def drain(chip, carry):
            for copy in outs(chip):
                copy.wait()
            return carry

        lax.fori_loop(0, chips, drain, 0)
    for swap in swaps:
        swap.wait()


def comm_call(
    number, own=None, part=None, tiles_of=None, weights=(), saved=(), n_made=0, swaps=()
):
    shards = lax.axis_size("shard")
    chips = shards // 2
    gathers, sums, heavy = own is not None, part is not None, tiles_of is not None
    ins, outs, scratch, sems = [], [], [], []
    width = own.shape[1] if gathers else part.shape[1]
    flops = 0
    moved = 0
    if gathers:
        rows = own.shape[0] * shards
        wide = jax.ShapeDtypeStruct((rows, width), BF16)
        ins.append(own)
        outs.append(wide)
        scratch.append(pltpu.VMEM((rows, width), BF16))
        moved += 30 * rows * width
    if heavy:
        ins += list(weights) + list(saved)
        units = weights[0].shape[0]
        thin = jax.ShapeDtypeStruct((rows, units), BF16)
        outs += [thin] * n_made + [wide]
        scratch += [pltpu.VMEM(x.shape, BF16) for x in ins[1:]]
        scratch += [pltpu.VMEM((rows, units), BF16)] * n_made
        scratch += [pltpu.VMEM((rows, width), BF16)]
        scratch += [pltpu.VMEM((2 * own.shape[0], width), F32)]
        flops = 6 * rows * units * width
    if sums:
        ins.append(part)
        size = part.shape[0] // shards
        outs.append(jax.ShapeDtypeStruct((size, width), F32))
        scratch.append(pltpu.VMEM((size, width), F32))
        scratch += [pltpu.VMEM((chips, size, width), BF16)] * 5
        moved += 30 * part.shape[0] * width
    dma = pltpu.SemaphoreType.DMA
    bits = tuple(bit for _, bit in swaps)
    ins += [x for x, _ in swaps]
    outs += [jax.ShapeDtypeStruct(x.shape, x.dtype) for x, _ in swaps]
    if gathers:
        sems += [dma((chips,))] * 5 + [dma]
    if sums:
        sems += [dma((chips,))] * 6 + [dma]
    if gathers:
        sems.append(dma((n_made + 2 if heavy else 1, chips)))
    if heavy:
        sems.append(dma((3 + len(saved),)))
    if bits:
        sems.append(dma((2, len(bits))))
    kernel = functools.partial(comm_kernel, tiles_of, len(saved), n_made, gathers, sums, bits)
    return pl.pallas_call(
        kernel,
        in_specs=[ANYWHERE] * len(ins),
        out_specs=[ANYWHERE] * len(outs),
        out_shape=outs,
        scratch_shapes=scratch + sems,
        compiler_params=pltpu.CompilerParams(
            collective_id=number, has_side_effects=True, vmem_limit_bytes=58 * 1024 * 1024
        ),
        cost_estimate=pl.CostEstimate(flops=flops, bytes_accessed=moved, transcendentals=0),
        name="comm%d" % number,
    )(*ins)


def over_tokens_kernel(a0, a1, b0, b1, c0, c1, x0, x1, g0, g1, out_ref):
    i = pl.program_id(0)
    tiles = pl.num_programs(0) // 3

    def product(l0, l1, r0, r1):
        out_ref[...] = (dot(l0[...], r0[...], TN) + dot(l1[...], r1[...], TN)).astype(BF16)

    @pl.when(i < tiles)
    def _():
        product(a0, a1, x0, x1)

    @pl.when((i >= tiles) & (i < 2 * tiles))
    def _():
        product(b0, b1, x0, x1)

    @pl.when(i >= 2 * tiles)
    def _():
        product(c0, c1, g0, g1)


def over_tokens(gates, ups, glus, xs, gs):
    rows, units = glus[0].shape
    width = xs[0].shape[1]
    tiles = units // FF_TILE
    whole = pl.BlockSpec((rows, width), lambda i: (0, 0), pipeline_mode=pl.Buffered(1))

    def some(n):
        return pl.BlockSpec((rows, FF_TILE), lambda i: (0, jnp.clip(i - n * tiles, 0, tiles - 1)))

    return pl.pallas_call(
        over_tokens_kernel,
        grid=(3 * tiles,),
        in_specs=[some(0), some(0), some(1), some(1), some(2), some(2)] + [whole] * 4,
        out_specs=pl.BlockSpec((FF_TILE, width), lambda i: (i, 0)),
        out_shape=jax.ShapeDtypeStruct((3 * units, width), BF16),
        compiler_params=kernel_params(),
        cost_estimate=pl.CostEstimate(
            flops=12 * rows * units * width, bytes_accessed=16 * rows * width, transcendentals=0
        ),
        name="over_tokens",
    )(*gates, *ups, *glus, *xs, *gs)


def swap_cores(x):
    n = lax.axis_size("shard")
    return lax.ppermute(x, "shard", [(s, s ^ 1) for s in range(n)])


def gather(x, axis_name, axis):
    return lax.all_gather(x, axis_name, axis=axis, tiled=True)


def scatter(x, axis_name, axis):
    return lax.psum_scatter(x, axis_name, scatter_dimension=axis, tiled=True)


def partner(x, bit):
    n = lax.axis_size("replica")
    return lax.ppermute(x, "replica", [(r, r ^ bit) for r in range(n)])


def halve_send(x, axis, bit):
    half = x.shape[axis] // 2
    mine = lax.rem(lax.axis_index("replica") // bit, 2)
    kept = lax.dynamic_slice_in_dim(x, mine * half, half, axis)
    sent = lax.dynamic_slice_in_dim(x, (1 - mine) * half, half, axis)
    return kept, partner(sent, bit)


def halve_sum(kept, got):
    return (kept.astype(F32) + got.astype(F32)).astype(BF16)


def halve(x, axis, bit):
    return halve_sum(*halve_send(x, axis, bit))


def join(x, other, axis, bit):
    mine = lax.rem(lax.axis_index("replica") // bit, 2) == 0
    return jnp.concatenate(
        [jnp.where(mine, x, other), jnp.where(mine, other, x)], axis=axis
    )


def double(x, axis, bit):
    return join(x, partner(x, bit), axis, bit)


class ReplicaSum:
    def __init__(self, x):
        half = x.shape[0] // 2
        self.kept = [x[:half], x[half:]]
        self.stage = 0

    def bits(self):
        return (1, 2) if self.stage in (0, 3) else (2, 1)

    def sends(self):
        pairs = []
        for n, bit in enumerate(self.bits()):
            x = self.kept[n]
            if self.stage < 2:
                half = x.shape[0] // 2
                mine = lax.rem(lax.axis_index("replica") // bit, 2)
                self.kept[n] = lax.dynamic_slice_in_dim(x, mine * half, half)
                x = lax.dynamic_slice_in_dim(x, (1 - mine) * half, half)
            pairs.append((x, bit))
        return pairs

    def receive(self, got):
        for n, (bit, other) in enumerate(zip(self.bits(), got)):
            if self.stage < 2:
                self.kept[n] = halve_sum(self.kept[n], other)
            else:
                self.kept[n] = join(self.kept[n], other, 0, bit)
        self.stage += 1

    def permute(self):
        self.receive([partner(x, bit) for x, bit in self.sends()])

    def result(self):
        return jnp.concatenate(self.kept).astype(F32)

    def thirds(self):
        first, second = self.kept
        third = (first.shape[0] + second.shape[0]) // 3
        rest = first.shape[0] - third
        middle = jnp.concatenate([first[third:], second[:rest]])
        return first[:third].astype(F32), middle.astype(F32), second[rest:].astype(F32)


def all_sends(sums):
    return [pair for one in sums for pair in one.sends()]


def all_receive(sums, got):
    for n, one in enumerate(sums):
        one.receive(got[2 * n : 2 * n + 2])


def sum_replicas(x):
    one = ReplicaSum(x)
    for _ in range(4):
        one.permute()
    return one.result()


def exchange(x):
    return lax.all_to_all(x, "shard", 0, 0, tiled=True)


def fast_on_device(
    tokens,
    w_query,
    w_key,
    w_value,
    w_output,
    gain_attn_in,
    gain_attn_out,
    gain_ffn_in,
    gain_ffn_out,
    w_gate,
    w_up,
    w_down,
    segment_ids,
    cotangent,
):
    tok_rows, width = tokens.shape
    w_rows = w_query.shape[0]
    shards = lax.axis_size("shard")
    replicas = lax.axis_size("replica")
    group_rows = tok_rows * shards
    shard_index = lax.axis_index("shard")
    first_core = lax.rem(shard_index, 2) == 0
    piece = w_rows // replicas

    x_group = gather(tokens, "shard", 0)
    gain_stack = jnp.stack([gain_attn_in, gain_attn_out, gain_ffn_in, gain_ffn_out])
    gains = gather(gain_stack, "shard", 1).astype(F32)

    start = lax.axis_index("replica") * piece
    wq = lax.dynamic_slice_in_dim(w_query, start, piece)
    wk = lax.dynamic_slice_in_dim(w_key, start, piece)
    wv = lax.dynamic_slice_in_dim(w_value, start, piece)
    sent = jnp.concatenate(
        [
            wq.reshape(piece, H, 2, 2, QUARTER).swapaxes(2, 3).reshape(piece, H, HD),
            wk.reshape(piece, KV, 2, 2, QUARTER).swapaxes(2, 3).reshape(piece, H, HALF),
            wv.reshape(piece, H, HALF),
        ],
        axis=2,
    ).swapaxes(0, 1)
    head_w = gather(exchange(sent), "replica", 1).reshape(width, 2 * HD)

    segment_row = segment_ids[0]
    smaller = jnp.sum((segment_row[:, None] < segment_row[None, :]).astype(jnp.int32), axis=0)
    earlier = jnp.concatenate([jnp.zeros((PROMPT,), jnp.int32), PROMPT + smaller])
    index = jnp.arange(group_rows, dtype=jnp.int32)
    low_row = earlier[None, :]
    positions = jnp.where(index < PROMPT, index, index - (earlier - PROMPT))
    rates = THETA ** (-(jnp.arange(HALF, dtype=F32) * 2.0) / HD)
    angles = positions.astype(F32)[:, None] * rates[None, :]
    cosine = jnp.cos(angles)
    sine = jnp.sin(angles)
    table = jnp.concatenate(
        [
            cosine[:, :QUARTER], cosine[:, :QUARTER], -sine[:, :QUARTER], sine[:, :QUARTER],
            cosine[:, QUARTER:], cosine[:, QUARTER:], -sine[:, QUARTER:], sine[:, QUARTER:],
        ],
        axis=1,
    )

    normed, queries, kv_own = qkv_call(x_group, gains[0:1], head_w, table)
    kv_other = swap_cores(kv_own)
    kv_low = jnp.where(first_core, kv_own, kv_other)
    kv_high = jnp.where(first_core, kv_other, kv_own)
    keys = jnp.concatenate([kv_low[:, :HALF], kv_high[:, :HALF]], axis=1)
    values = jnp.concatenate([kv_low[:, HALF:], kv_high[:, HALF:]], axis=1)
    attended, lse, raw_top, raw_end = attend_call(queries, keys, values, low_row, w_output)
    x_float = tokens.astype(F32)
    grad_top = cotangent.astype(F32)
    chunks = 2
    size = tok_rows // chunks

    weights = (w_gate, w_up, w_down)
    (raw_first,) = comm_call(0, part=raw_top)

    def enter(raw, c):
        hidden = x_float[c * size : (c + 1) * size] + rms_scaled(raw, gains[1])
        return hidden, rms_scaled(hidden, gains[2]).astype(BF16)

    def leave(raw, hidden, c):
        out = (hidden + rms_scaled(raw, gains[3])).astype(BF16)
        _, pull = jax.vjp(rms_scaled, raw, gains[3])
        d_raw, gain_term = pull(grad_top[c * size : (c + 1) * size])
        return out, d_raw.astype(BF16), gain_term

    hidden_first, low_first = enter(raw_first, 0)
    normed_0, gate_0, up_0, glu_0, part_0, raw_second = comm_call(
        1, low_first, raw_end, forward_tiles, weights, n_made=3
    )
    hidden_second, low_second = enter(raw_second, 1)
    normed_1, gate_1, up_1, glu_1, part_1, ffn_first = comm_call(
        1, low_second, part_0, forward_tiles, weights, n_made=3
    )
    out_first, d_first, g4_first = leave(ffn_first, hidden_first, 0)
    d_all_0, d_gate_0, d_up_0, d_part_0, ffn_second = comm_call(
        2, d_first, part_1, backward_tiles, weights, (gate_0, up_0), n_made=2
    )
    out_second, d_second, g4_second = leave(ffn_second, hidden_second, 1)
    d_all_1, d_gate_1, d_up_1, d_part_1, d_normed_first = comm_call(
        2, d_second, d_part_0, backward_tiles, weights, (gate_1, up_1), n_made=2
    )
    glus, d_groups = (glu_0, glu_1), (d_all_0, d_all_1)
    d_gates, d_ups, normed_groups = (d_gate_0, d_gate_1), (d_up_0, d_up_1), (normed_0, normed_1)
    hidden_parts, raw_parts = (hidden_first, hidden_second), (raw_first, raw_second)
    outs, gain_four = (out_first, out_second), (g4_first, g4_second)

    sums = [ReplicaSum(over_tokens(d_gates, d_ups, glus, normed_groups, d_groups))]

    def back(d_normed, c):
        rows = slice(c * size, (c + 1) * size)
        _, pull = jax.vjp(rms_scaled, hidden_parts[c], gains[2])
        part, g3 = pull(d_normed)
        d_hidden = grad_top[rows] + part
        _, pull = jax.vjp(rms_scaled, raw_parts[c], gains[1])
        d_raw, g2 = pull(d_hidden)
        return d_hidden, d_raw.astype(BF16), g2, g3

    d_hidden_first, d_attn_first, g2_first, g3_first = back(d_normed_first, 0)
    d_attn_0, d_normed_second, *got = comm_call(
        3, d_attn_first, d_part_1, swaps=all_sends(sums)
    )
    all_receive(sums, got)
    d_hidden_second, d_attn_second, g2_second, g3_second = back(d_normed_second, 1)
    d_attn_1, *got = comm_call(4, d_attn_second, swaps=all_sends(sums))
    all_receive(sums, got)
    d_hidden = jnp.concatenate([d_hidden_first, d_hidden_second])
    gain_two, gain_three = (g2_first, g2_second), (g3_first, g3_second)
    dq, dk, dv, grad_out, *got = attend_back_call(
        6, queries, keys, values, low_row, lse, attended, d_attn_0, d_attn_1, w_output, table,
        all_sends(sums),
    )
    all_receive(sums, got)
    dkv_low = jnp.concatenate([dk[:, :HALF], dv[:, :HALF]], axis=1)
    dkv_high = jnp.concatenate([dk[:, HALF:], dv[:, HALF:]], axis=1)
    dkv_mine = jnp.where(first_core, dkv_low, dkv_high).astype(F32)
    dkv = dkv_mine + swap_cores(jnp.where(first_core, dkv_high, dkv_low)).astype(F32)
    dk_half = dkv[:, :HALF]
    own = jnp.where(first_core, table[:, :HD], table[:, HD:])
    turned = jnp.concatenate([dk_half[:, QUARTER:], dk_half[:, :QUARTER]], axis=1)
    dk_lin = dk_half * own[:, :HALF] - turned * own[:, HALF:]
    d_lin = jnp.concatenate([dq, dk_lin.astype(BF16), dkv[:, HALF:].astype(BF16)], axis=1)
    part, d_lin = lax.optimization_barrier((dot(d_lin, head_w, NT).astype(BF16), d_lin))
    d_normed, *got = comm_call(5, part=part, swaps=all_sends(sums))
    all_receive(sums, got)
    grad_head = dot(normed, d_lin, TN)
    gain_one = jnp.sum(grad_head * head_w.astype(F32), axis=1) / gains[0]
    _, pull = jax.vjp(rms_scaled, x_float, gains[0])
    input_grad = d_hidden + pull(d_normed)[0]

    gain_terms = jnp.stack([gain_one, sum(gain_two), sum(gain_three), sum(gain_four)], axis=1)
    padded = jnp.pad(gain_terms, ((0, 0), (0, HALF - gain_terms.shape[1])))
    moved = jnp.concatenate([grad_head, padded], axis=1).astype(BF16)
    moved = moved.reshape(shards, w_rows, moved.shape[1])
    cut = HD + HALF
    left = halve(halve(moved[:, :, :cut], 1, 1), 1, 2)
    right = halve(halve(moved[:, :, cut:], 1, 2), 1, 1)
    traded = exchange(jnp.concatenate([left, right], axis=2))
    left = double(double(traded[:, :, :cut], 1, 2), 1, 1).astype(F32)
    right = double(double(traded[:, :, cut:], 1, 1), 1, 2).astype(F32)
    grad_query = (
        left[:, :, :HD].reshape(H, w_rows, 2, 2, QUARTER).transpose(1, 0, 3, 2, 4)
    ).reshape(w_rows, H * HD)
    grad_key = (
        left[:, :, HD:]
        .reshape(KV, 2, w_rows, 2, QUARTER)
        .transpose(2, 0, 3, 1, 4)
        .reshape(w_rows, KV * HD)
    )
    grad_value = right[:, :, :HALF].transpose(1, 0, 2).reshape(w_rows, KV * HD)
    grad_out_proj = sum_replicas(grad_out)
    grad_gate, grad_up, grad_down = sums[0].thirds()
    gain_shares = jnp.sum(right[:, :, HALF : HALF + gain_terms.shape[1]], axis=0).T
    return (
        jnp.concatenate(outs),
        input_grad,
        grad_query,
        grad_key,
        grad_value,
        grad_out_proj,
        gain_shares[0],
        gain_shares[1],
        gain_shares[2],
        gain_shares[3],
        grad_gate,
        grad_up,
        grad_down,
    )


def solution(mesh):
    placed = (
        P(("replica", "shard"), None),
        P("shard", None),
        P("shard", None),
        P("shard", None),
        P("shard", None),
        P("shard"),
        P("shard"),
        P("shard"),
        P("shard"),
        P("shard", None),
        P("shard", None),
        P("shard", None),
        P("replica", None),
        P(("replica", "shard"), None),
    )
    heads_fit = mesh.shape["shard"] == H and H == 2 * KV and mesh.shape["replica"] == 4
    body = fast_on_device if heads_fit else on_device
    return jax.shard_map(
        body,
        mesh=mesh,
        in_specs=placed,
        out_specs=(
            P(("replica", "shard"), None),
            P(("replica", "shard"), None),
            P("shard", None),
            P("shard", None),
            P("shard", None),
            P("shard", None),
            P("shard"),
            P("shard"),
            P("shard"),
            P("shard"),
            P("shard", None),
            P("shard", None),
            P("shard", None),
        ),
        check_vma=False,
    )
```

```python
import functools

import jax
import jax.numpy as jnp
from jax import lax
from jax.experimental import pallas as pl
from jax.experimental.pallas import tpu as pltpu
from jax.sharding import PartitionSpec as P

H = 8
KV = 4
HD = 256
PROMPT = 1024


EPS = 1e-06
CAP = 50.0
THETA = 10000.0
NEGATIVE = -1e30


def inv_rms(values):
    return lax.rsqrt(jnp.mean(values * values, axis=-1, keepdims=True) + EPS)


def rms_scaled(values, gain):
    return values * inv_rms(values) * gain


def rotate(values, positions, head_count, head_dim, sign):
    tok_count = values.shape[0]
    half = head_dim // 2
    rates = THETA ** (-(jnp.arange(half, dtype=jnp.float32) * 2.0) / head_dim)
    angles = positions.astype(jnp.float32)[:, None] * rates[None, :]
    cosine = jnp.cos(angles)[:, None, :]
    sine = sign * jnp.sin(angles)[:, None, :]
    shaped = values.reshape(tok_count, head_count, head_dim)
    first = shaped[:, :, :half]
    second = shaped[:, :, half:]
    turned = jnp.concatenate(
        [first * cosine - second * sine, second * cosine + first * sine], axis=-1
    )
    return turned.reshape(tok_count, head_count * head_dim)


def glu_value(gate, up):
    return jax.nn.gelu(gate, approximate=True) * up


def on_device(
    tokens,
    w_query,
    w_key,
    w_value,
    w_output,
    gain_attn_in,
    gain_attn_out,
    gain_ffn_in,
    gain_ffn_out,
    w_gate,
    w_up,
    w_down,
    segment_ids,
    cotangent,
):
    tok_rows = tokens.shape[0]
    query_cols = w_query.shape[1]
    kv_cols = w_key.shape[1]
    group_rows = tok_rows * lax.axis_size("shard")
    head_group = H // KV
    shard_index = lax.axis_index("shard")
    start_row = shard_index * tok_rows
    segment_row = segment_ids[0]
    key_segments = jnp.concatenate([jnp.full((PROMPT,), -1, jnp.int32), segment_row])
    key_index = jnp.arange(group_rows, dtype=jnp.int32)
    query_index = start_row + jnp.arange(tok_rows, dtype=jnp.int32)
    query_segments = lax.dynamic_slice_in_dim(key_segments, start_row, tok_rows)
    earlier = jnp.sum((segment_row[None, :] < query_segments[:, None]).astype(jnp.int32), axis=1)
    positions = query_index - earlier
    visible = (key_index[None, :] <= query_index[:, None]) & (
        (key_index[None, :] < PROMPT) | (key_segments[None, :] == query_segments[:, None])
    )
    gain_stack = jnp.stack([gain_attn_in, gain_attn_out, gain_ffn_in, gain_ffn_out])
    full_query, full_key, full_value, full_out, gains = (
        lax.all_gather(w_query, "shard", axis=0, tiled=True),
        lax.all_gather(w_key, "shard", axis=0, tiled=True),
        lax.all_gather(w_value, "shard", axis=0, tiled=True),
        lax.all_gather(w_output, "shard", axis=0, tiled=True),
        lax.all_gather(gain_stack, "shard", axis=1, tiled=True),
    )
    gain_first = gains[0].astype(jnp.float32)
    gain_second = gains[1].astype(jnp.float32)
    gain_third = gains[2].astype(jnp.float32)
    gain_fourth = gains[3].astype(jnp.float32)
    x_float = tokens.astype(jnp.float32)
    normed = rms_scaled(x_float, gain_first).astype(jnp.bfloat16)
    query_lin = jnp.dot(normed, full_query, preferred_element_type=jnp.float32)
    key_lin = jnp.dot(normed, full_key, preferred_element_type=jnp.float32)
    value_lin = jnp.dot(normed, full_value, preferred_element_type=jnp.float32)
    query_scale = HD ** (-0.5)
    queries = (rotate(query_lin, positions, H, HD, 1.0) * query_scale).astype(jnp.bfloat16)
    keys = rotate(key_lin, positions, KV, HD, 1.0).astype(jnp.bfloat16)
    values = value_lin.astype(jnp.bfloat16)
    group_keys, group_values = (
        lax.all_gather(keys, "shard", axis=0, tiled=True),
        lax.all_gather(values, "shard", axis=0, tiled=True),
    )
    keys_shaped = group_keys.reshape(group_rows, KV, HD)
    values_shaped = group_values.reshape(group_rows, KV, HD)
    query_shaped = queries.reshape(tok_rows, KV, head_group, HD)

    def capped_scores():
        scores = jnp.einsum(
            "qkgd,pkd->kgqp", query_shaped, keys_shaped, preferred_element_type=jnp.float32
        )
        bent = jnp.tanh(scores / CAP)
        return (bent, jnp.where(visible[None, None], CAP * bent, NEGATIVE))

    bent, capped = capped_scores()
    highest = jnp.max(capped, axis=-1, keepdims=True)
    log_total = highest + jnp.log(jnp.sum(jnp.exp(capped - highest), axis=-1, keepdims=True))
    probs = jnp.exp(capped - log_total)
    probs_low = probs.astype(jnp.bfloat16)
    attended = jnp.einsum(
        "kgqp,pkd->qkgd", probs_low, values_shaped, preferred_element_type=jnp.float32
    )
    attended_low = attended.reshape(tok_rows, query_cols).astype(jnp.bfloat16)
    raw_attn = jnp.dot(attended_low, full_out, preferred_element_type=jnp.float32)
    hidden_state = x_float + rms_scaled(raw_attn, gain_second)
    normed_ffn = rms_scaled(hidden_state, gain_third).astype(jnp.bfloat16)
    group_normed = lax.all_gather(normed_ffn, "shard", axis=0, tiled=True)
    gate = jnp.einsum("td,fd->tf", group_normed, w_gate, preferred_element_type=jnp.float32)
    up = jnp.einsum("td,fd->tf", group_normed, w_up, preferred_element_type=jnp.float32)
    glu = glu_value(gate, up).astype(jnp.bfloat16)
    raw_ffn = lax.psum_scatter(
        jnp.dot(glu, w_down, preferred_element_type=jnp.float32).astype(jnp.bfloat16),
        "shard",
        scatter_dimension=0,
        tiled=True,
    ).astype(jnp.float32)
    output = (hidden_state + rms_scaled(raw_ffn, gain_fourth)).astype(jnp.bfloat16)
    grad_top = cotangent.astype(jnp.float32)
    _, pull_fourth = jax.vjp(rms_scaled, raw_ffn, gain_fourth)
    d_raw_ffn, grad_gain_fourth = pull_fourth(grad_top)
    d_raw_low = d_raw_ffn.astype(jnp.bfloat16)
    group_d_raw = lax.all_gather(d_raw_low, "shard", axis=0, tiled=True)
    grad_down = jnp.einsum("tf,td->fd", glu, group_d_raw, preferred_element_type=jnp.float32)
    d_glu = jnp.einsum("td,fd->tf", group_d_raw, w_down, preferred_element_type=jnp.float32)
    _, pull_glu = jax.vjp(glu_value, gate, up)
    d_gate, d_up = pull_glu(d_glu)
    d_gate_low = d_gate.astype(jnp.bfloat16)
    d_up_low = d_up.astype(jnp.bfloat16)
    grad_gate = jnp.einsum(
        "tf,td->fd", d_gate_low, group_normed, preferred_element_type=jnp.float32
    )
    grad_up = jnp.einsum("tf,td->fd", d_up_low, group_normed, preferred_element_type=jnp.float32)
    gate_part = jnp.dot(d_gate_low, w_gate, preferred_element_type=jnp.float32)
    up_part = jnp.dot(d_up_low, w_up, preferred_element_type=jnp.float32)
    d_normed_ffn = lax.psum_scatter(
        (gate_part + up_part).astype(jnp.bfloat16), "shard", scatter_dimension=0, tiled=True
    ).astype(jnp.float32)
    _, pull_third = jax.vjp(rms_scaled, hidden_state, gain_third)
    d_hidden_part, grad_gain_third = pull_third(d_normed_ffn)
    d_hidden = grad_top + d_hidden_part
    _, pull_second = jax.vjp(rms_scaled, raw_attn, gain_second)
    d_raw_attn, grad_gain_second = pull_second(d_hidden)
    d_raw_attn_low = d_raw_attn.astype(jnp.bfloat16)
    picked = attended_low
    grad_out_proj = lax.psum_scatter(
        jnp.einsum("tf,td->fd", picked, d_raw_attn_low, preferred_element_type=jnp.float32).astype(
            jnp.bfloat16
        ),
        "shard",
        scatter_dimension=0,
        tiled=True,
    ).astype(jnp.float32)
    d_attended_low = jnp.einsum(
        "td,fd->tf", d_raw_attn_low, full_out, preferred_element_type=jnp.float32
    ).astype(jnp.bfloat16)
    d_attended_shaped = d_attended_low.reshape(tok_rows, KV, head_group, HD)
    bent_again, capped_again = capped_scores()
    probs_again = jnp.exp(capped_again - log_total)
    probs_again_low = probs_again.astype(jnp.bfloat16)
    d_probs = jnp.einsum(
        "qkgd,pkd->kgqp", d_attended_shaped, values_shaped, preferred_element_type=jnp.float32
    )
    d_capped = probs_again * (d_probs - jnp.sum(probs_again * d_probs, axis=-1, keepdims=True))
    d_scores_low = (d_capped * (1.0 - bent_again * bent_again)).astype(jnp.bfloat16)
    d_queries = jnp.einsum(
        "kgqp,pkd->qkgd", d_scores_low, keys_shaped, preferred_element_type=jnp.float32
    ).reshape(tok_rows, query_cols)
    d_keys_group = jnp.einsum(
        "kgqp,qkgd->pkd", d_scores_low, query_shaped, preferred_element_type=jnp.float32
    ).reshape(group_rows, kv_cols)
    d_values_group = jnp.einsum(
        "kgqp,qkgd->pkd", probs_again_low, d_attended_shaped, preferred_element_type=jnp.float32
    ).reshape(group_rows, kv_cols)
    d_keys, d_values = (
        lax.psum_scatter(
            d_keys_group.astype(jnp.bfloat16), "shard", scatter_dimension=0, tiled=True
        ).astype(jnp.float32),
        lax.psum_scatter(
            d_values_group.astype(jnp.bfloat16), "shard", scatter_dimension=0, tiled=True
        ).astype(jnp.float32),
    )
    d_query_low = rotate(d_queries * query_scale, positions, H, HD, -1.0).astype(jnp.bfloat16)
    d_key_low = rotate(d_keys, positions, KV, HD, -1.0).astype(jnp.bfloat16)
    d_value_low = d_values.astype(jnp.bfloat16)
    d_normed = jnp.einsum("tf,df->td", d_query_low, full_query, preferred_element_type=jnp.float32)
    d_normed = d_normed + jnp.einsum(
        "tf,df->td", d_key_low, full_key, preferred_element_type=jnp.float32
    )
    d_normed = d_normed + jnp.einsum(
        "tf,df->td", d_value_low, full_value, preferred_element_type=jnp.float32
    )
    _, pull_first = jax.vjp(rms_scaled, x_float, gain_first)
    d_input_part, grad_gain_first = pull_first(d_normed)
    input_grad = d_hidden + d_input_part
    d_projected = jnp.concatenate([d_query_low, d_key_low, d_value_low], axis=1)
    picked = normed
    grad_projected = lax.psum_scatter(
        jnp.einsum("tc,tf->cf", picked, d_projected, preferred_element_type=jnp.float32).astype(
            jnp.bfloat16
        ),
        "shard",
        scatter_dimension=0,
        tiled=True,
    ).astype(jnp.float32)
    grad_query = grad_projected[:, :query_cols]
    grad_key = grad_projected[:, query_cols : query_cols + kv_cols]
    grad_value = grad_projected[:, query_cols + kv_cols :]
    gain_terms = jnp.stack([grad_gain_first, grad_gain_second, grad_gain_third, grad_gain_fourth])
    gain_shares = lax.psum_scatter(
        gain_terms.astype(jnp.bfloat16), "shard", scatter_dimension=1, tiled=True
    ).astype(jnp.float32)
    grad_query, grad_key, grad_value, grad_out_proj, gain_shares, grad_gate, grad_up, grad_down = (
        lax.psum(grad_query.astype(jnp.bfloat16), "replica").astype(jnp.float32),
        lax.psum(grad_key.astype(jnp.bfloat16), "replica").astype(jnp.float32),
        lax.psum(grad_value.astype(jnp.bfloat16), "replica").astype(jnp.float32),
        lax.psum(grad_out_proj.astype(jnp.bfloat16), "replica").astype(jnp.float32),
        lax.psum(gain_shares.astype(jnp.bfloat16), "replica").astype(jnp.float32),
        lax.psum(grad_gate.astype(jnp.bfloat16), "replica").astype(jnp.float32),
        lax.psum(grad_up.astype(jnp.bfloat16), "replica").astype(jnp.float32),
        lax.psum(grad_down.astype(jnp.bfloat16), "replica").astype(jnp.float32),
    )
    return (
        output,
        input_grad,
        grad_query,
        grad_key,
        grad_value,
        grad_out_proj,
        gain_shares[0],
        gain_shares[1],
        gain_shares[2],
        gain_shares[3],
        grad_gate,
        grad_up,
        grad_down,
    )


BLOCK = 256
HALF = HD // 2
QUARTER = HD // 4
NT = (((1,), (1,)), ((), ()))
TN = (((0,), (0,)), ((), ()))
F32 = jnp.float32
BF16 = jnp.bfloat16


def dot(a, b, dims=(((1,), (0,)), ((), ()))):
    return lax.dot_general(a, b, dims, preferred_element_type=F32)


def turn(x, cosine, sine):
    return x * cosine + pltpu.roll(x, QUARTER, 1) * sine


def qkv_kernel(x_ref, gain_ref, w_ref, tab_ref, normed_ref, q_ref, kv_ref):
    core = lax.rem(lax.axis_index("shard"), 2)
    x = x_ref[...].astype(F32)
    normed = (x * inv_rms(x) * gain_ref[...]).astype(BF16)
    normed_ref[...] = normed
    lin = dot(normed, w_ref[...])
    tab = tab_ref[...]
    c0, s0, c1, s1 = (tab[:, i * HALF : (i + 1) * HALF] for i in range(4))
    scale = HD ** (-0.5)
    q_ref[:, :HALF] = (turn(lin[:, :HALF], c0, s0) * scale).astype(BF16)
    q_ref[:, HALF:] = (turn(lin[:, HALF:HD], c1, s1) * scale).astype(BF16)
    first = core == 0
    ck = jnp.where(first, c0, c1)
    sk = jnp.where(first, s0, s1)
    kv_ref[:, :HALF] = turn(lin[:, HD : HD + HALF], ck, sk).astype(BF16)
    kv_ref[:, HALF:] = lin[:, HD + HALF :].astype(BF16)


def visible_block(low_row, i, j):
    key = j * BLOCK + lax.broadcasted_iota(jnp.int32, (BLOCK, BLOCK), 0)
    query = i * BLOCK + lax.broadcasted_iota(jnp.int32, (BLOCK, BLOCK), 1)
    return (key <= query) & (key >= low_row)


def block_ranges(i):
    whole = PROMPT // BLOCK
    full = jnp.minimum(i, whole)
    return full, full, i + 1


def attend_kernel(q_ref, k_ref, v_ref, low_ref, wo_ref, att_ref, lse_ref, top_ref, end_ref):
    i = pl.program_id(0)
    q = q_ref[...]
    low_row = low_ref[...]

    def step(j, carry, masked):
        acc, total = carry
        rows = pl.ds(pl.multiple_of(j * BLOCK, BLOCK), BLOCK)
        s = dot(k_ref[rows, :], q, NT)
        p = jnp.exp(CAP * jnp.tanh(s * (1.0 / CAP)))
        if masked:
            p = jnp.where(visible_block(low_row, i, j), p, 0.0)
        total = total + jnp.sum(p, axis=0, keepdims=True)
        acc = acc + dot(v_ref[rows, :], p.astype(BF16), TN)
        return acc, total

    full, start, stop = block_ranges(i)
    carry = (jnp.zeros((HD, BLOCK), F32), jnp.zeros((1, BLOCK), F32))
    carry = lax.fori_loop(0, full, functools.partial(step, masked=False), carry)
    acc, total = lax.fori_loop(start, stop, functools.partial(step, masked=True), carry)
    lse_ref[...] = jnp.log(total)
    att = (acc / total).T.astype(BF16)
    att_ref[...] = att
    part = dot(att, wo_ref[...]).astype(BF16)
    top_ref[...] = part[: BLOCK // 2]
    end_ref[...] = part[BLOCK // 2 :]


def swap_copies(sources, targets, bits, sems):
    return [
        pltpu.make_async_remote_copy(
            src_ref=src,
            dst_ref=dst,
            send_sem=sems.at[0, n],
            recv_sem=sems.at[1, n],
            device_id={"replica": flipped(bit)},
            device_id_type=pl.DeviceIdType.MESH,
        )
        for n, (src, dst, bit) in enumerate(zip(sources, targets, bits))
    ]


def attend_back_kernel(
    q_ref, k_ref, v_ref, low_ref, lse_ref, att_ref, top_ref, end_ref, wo_ref, tab_ref,
    dq_ref, dk_ref, dv_ref, go_ref, dk_acc, dv_acc, go_acc,
):
    i = pl.program_id(0)

    @pl.when(i == 0)
    def _():
        dk_acc[...] = jnp.zeros_like(dk_acc)
        dv_acc[...] = jnp.zeros_like(dv_acc)
        go_acc[...] = jnp.zeros_like(go_acc)

    q = q_ref[...]
    g = jnp.concatenate([top_ref[...], end_ref[...]])
    att = att_ref[...]
    low_row = low_ref[...]
    lse_row = lse_ref[...]
    go_acc[...] += dot(att, g, TN)
    da = dot(g, wo_ref[...], NT).astype(BF16)
    weighted = da.astype(F32) * att.astype(F32)
    d_row = jnp.sum(weighted.T, axis=0, keepdims=True)

    def step(j, dq, masked):
        rows = pl.ds(pl.multiple_of(j * BLOCK, BLOCK), BLOCK)
        k = k_ref[rows, :]
        bent = jnp.tanh(dot(k, q, NT) * (1.0 / CAP))
        p = jnp.exp(CAP * bent - lse_row)
        if masked:
            p = jnp.where(visible_block(low_row, i, j), p, 0.0)
        dp = dot(v_ref[rows, :], da, NT)
        ds = (p * (dp - d_row) * (1.0 - bent * bent)).astype(BF16)
        dk_acc[rows, :] += dot(ds, q)
        dv_acc[rows, :] += dot(p.astype(BF16), da)
        return dq + dot(ds, k, TN)

    full, start, stop = block_ranges(i)
    dq = jnp.zeros((BLOCK, HD), F32)
    dq = lax.fori_loop(0, full, functools.partial(step, masked=False), dq)
    dq = lax.fori_loop(start, stop, functools.partial(step, masked=True), dq)
    dq = dq * HD ** (-0.5)
    tab = tab_ref[...]
    c0, s0, c1, s1 = (tab[:, n * HALF : (n + 1) * HALF] for n in range(4))
    dq_ref[:, :HALF] = turn(dq[:, :HALF], c0, -s0).astype(BF16)
    dq_ref[:, HALF:] = turn(dq[:, HALF:], c1, -s1).astype(BF16)

    @pl.when(i == pl.num_programs(0) - 1)
    def _():
        dk_ref[...] = dk_acc[...].astype(BF16)
        dv_ref[...] = dv_acc[...].astype(BF16)
        go_ref[...] = go_acc[...].astype(BF16)


ANYWHERE = pl.BlockSpec(memory_space=pl.ANY)


def rows_spec(cols):
    return pl.BlockSpec((BLOCK, cols), lambda i: (i, 0))


def half_spec(cols):
    return pl.BlockSpec((BLOCK // 2, cols), lambda i: (i, 0))


def whole_spec(rows, cols):
    return pl.BlockSpec((rows, cols), lambda i: (0, 0))


def lane_spec():
    return pl.BlockSpec((1, BLOCK), lambda i: (0, i))


def kernel_params():
    return pltpu.CompilerParams(
        dimension_semantics=("arbitrary",), vmem_limit_bytes=48 * 1024 * 1024
    )


def qkv_call(x, gain, weights, table):
    rows, width = x.shape
    cols = weights.shape[1]
    return pl.pallas_call(
        qkv_kernel,
        grid=(rows // BLOCK,),
        in_specs=[rows_spec(width), whole_spec(1, width), whole_spec(width, cols), rows_spec(cols)],
        out_specs=[rows_spec(width), rows_spec(HD), rows_spec(HD)],
        out_shape=[
            jax.ShapeDtypeStruct((rows, width), BF16),
            jax.ShapeDtypeStruct((rows, HD), BF16),
            jax.ShapeDtypeStruct((rows, HD), BF16),
        ],
        compiler_params=kernel_params(),
        cost_estimate=pl.CostEstimate(
            flops=2 * rows * width * cols, bytes_accessed=4 * rows * width, transcendentals=0
        ),
        name="qkv",
    )(x, gain, weights, table)


def attend_call(q, k, v, low_row, wo):
    rows = q.shape[0]
    width = wo.shape[1]
    return pl.pallas_call(
        attend_kernel,
        grid=(rows // BLOCK,),
        in_specs=[
            rows_spec(HD), whole_spec(rows, HD), whole_spec(rows, HD), lane_spec(),
            whole_spec(HD, width),
        ],
        out_specs=[rows_spec(HD), lane_spec(), half_spec(width), half_spec(width)],
        out_shape=[
            jax.ShapeDtypeStruct((rows, HD), BF16),
            jax.ShapeDtypeStruct((1, rows), F32),
            jax.ShapeDtypeStruct((rows // 2, width), BF16),
            jax.ShapeDtypeStruct((rows // 2, width), BF16),
        ],
        compiler_params=kernel_params(),
        cost_estimate=pl.CostEstimate(
            flops=3 * rows * rows * HD + 2 * rows * width * HD,
            bytes_accessed=2 * rows * width,
            transcendentals=rows * rows,
        ),
        name="attend",
    )(q, k, v, low_row, wo)


def attend_back_call(q, k, v, low_row, lse, att, top, end, wo, table):
    rows = q.shape[0]
    width = wo.shape[1]
    return pl.pallas_call(
        attend_back_kernel,
        grid=(rows // BLOCK,),
        in_specs=[
            rows_spec(HD), whole_spec(rows, HD), whole_spec(rows, HD), lane_spec(), lane_spec(),
            rows_spec(HD), half_spec(width), half_spec(width), whole_spec(HD, width),
            rows_spec(4 * HALF),
        ],
        out_specs=[
            rows_spec(HD), whole_spec(rows, HD), whole_spec(rows, HD), whole_spec(HD, width),
        ],
        out_shape=[
            jax.ShapeDtypeStruct((rows, HD), BF16),
            jax.ShapeDtypeStruct((rows, HD), BF16),
            jax.ShapeDtypeStruct((rows, HD), BF16),
            jax.ShapeDtypeStruct((HD, width), BF16),
        ],
        scratch_shapes=[
            pltpu.VMEM((rows, HD), F32),
            pltpu.VMEM((rows, HD), F32),
            pltpu.VMEM((HD, width), F32),
        ],
        compiler_params=kernel_params(),
        cost_estimate=pl.CostEstimate(
            flops=6 * rows * rows * HD + 4 * rows * width * HD,
            bytes_accessed=2 * rows * width,
            transcendentals=rows * rows,
        ),
        name="attend_back",
    )(q, k, v, low_row, lse, att, top, end, wo, table)


def gelu_parts(v):
    k = (2.0 / jnp.pi) ** 0.5
    square = v * v
    bent = jnp.tanh(k * v * (1.0 + 0.044715 * square))
    half = 0.5 * (1.0 + bent)
    slope = half + 0.5 * v * (1.0 - bent * bent) * k * (1.0 + 3 * 0.044715 * square)
    return v * half, slope


def flipped(bit):
    r = lax.axis_index("replica")
    return r + bit * (1 - 2 * lax.rem(r // bit, 2))


def greet_neighbours(chips, bits=()):
    barrier = pltpu.get_barrier_semaphore()
    for bit in bits:
        pl.semaphore_signal(
            barrier,
            inc=1,
            device_id={"replica": flipped(bit)},
            device_id_type=pl.DeviceIdType.MESH,
        )
    me = lax.axis_index("shard")
    z, core, last = me // 2, lax.rem(me, 2), chips - 1

    def greet(chip, other):
        pl.semaphore_signal(
            barrier,
            inc=1,
            device_id={"shard": chip * 2 + other},
            device_id_type=pl.DeviceIdType.MESH,
        )

    greet(z, 1 - core)

    @pl.when(z > 0)
    def _():
        greet(z - 1, core)

    @pl.when(z < last)
    def _():
        greet(z + 1, core)

    pl.semaphore_wait(barrier, 1 + len(bits) + jnp.minimum(z, 1) + jnp.minimum(last - z, 1))


class Line:
    def __init__(self, own, buf, sems, chips):
        self.own, self.buf, self.chips = own, buf, chips
        self.right, self.left, self.side, self.got, self.got_side = sems
        me = lax.axis_index("shard")
        self.z, self.core = me // 2, lax.rem(me, 2)
        self.rows = own.shape[0]

    def place(self, chip, core):
        first = pl.multiple_of((chip * 2 + core) * self.rows, self.rows)
        return self.buf.at[pl.ds(first, self.rows)]

    def move(self, chip, src, send, got, target_chip, target_core):
        return pltpu.make_async_remote_copy(
            src_ref=src,
            dst_ref=self.place(chip, self.core),
            send_sem=send.at[chip],
            recv_sem=got.at[chip],
            device_id={"shard": target_chip * 2 + target_core},
            device_id_type=pl.DeviceIdType.MESH,
        )

    def to_right(self, chip, src):
        return self.move(chip, src, self.right, self.got, self.z + 1, self.core)

    def to_left(self, chip, src):
        return self.move(chip, src, self.left, self.got, self.z - 1, self.core)

    def to_side(self, chip, src):
        return self.move(chip, src, self.side, self.got_side, self.z, 1 - self.core)

    def start(self):
        z, last = self.z, self.chips - 1

        @pl.when(z > 0)
        def _():
            self.to_left(z, self.own).start()

        @pl.when(z < last)
        def _():
            self.to_right(z, self.own).start()

        self.to_side(z, self.own).start()

    def pass_on(self, hop):
        z, last = self.z, self.chips - 1

        @pl.when((hop > 0) & (z >= hop))
        def _():
            chip = z - hop
            block = self.place(chip, self.core)
            self.to_right(chip, block).wait_recv()

            @pl.when(z < last)
            def _():
                self.to_right(chip, block).start()

            self.to_side(chip, block).start()

        @pl.when((hop > 0) & (z + hop <= last))
        def _():
            chip = z + hop
            block = self.place(chip, self.core)
            self.to_left(chip, block).wait_recv()

            @pl.when(z > 0)
            def _():
                self.to_left(chip, block).start()

            self.to_side(chip, block).start()

    def chip_at(self, step):
        z = self.z
        near = z + 1 - 2 * lax.rem(z, 2)
        high = z // 2
        by_step = (z, near, 2 - high, 3 - 3 * high)
        chip = by_step[0]
        for n in range(1, 4):
            chip = jnp.where(step == n, by_step[n], chip)
        return chip

    def wait_side(self, chip):
        pltpu.make_async_remote_copy(
            src_ref=self.place(chip, self.core),
            dst_ref=self.place(chip, 1 - self.core),
            send_sem=self.side.at[chip],
            recv_sem=self.got_side.at[chip],
            device_id={"shard": self.z * 2 + 1 - self.core},
            device_id_type=pl.DeviceIdType.MESH,
        ).wait_recv()

    def finish(self):
        z, last = self.z, self.chips - 1

        def done(chip, carry):
            @pl.when((z < last) & (chip <= z))
            def _():
                self.to_right(chip, self.place(chip, self.core)).wait_send()

            @pl.when((z > 0) & (chip >= z))
            def _():
                self.to_left(chip, self.place(chip, self.core)).wait_send()

            self.to_side(chip, self.place(chip, self.core)).wait_send()
            return carry

        lax.fori_loop(0, self.chips, done, 0)


class Chain:
    def __init__(self, part, total, total_hbm, bufs, sems, chips):
        self.part, self.total, self.total_hbm, self.chips = part, total, total_hbm, chips
        self.mine, self.side, self.from_left, self.from_right, self.stage = bufs
        (
            self.mine_sem, self.side_send, self.side_got, self.sent, self.left_got,
            self.right_got, self.total_sem,
        ) = sems
        me = lax.axis_index("shard")
        self.z, self.core = me // 2, lax.rem(me, 2)
        self.rows = self.mine.shape[1]

    def block(self, chip, core):
        first = pl.multiple_of((chip * 2 + core) * self.rows, self.rows)
        return self.part.at[pl.ds(first, self.rows)]

    def load(self, chip):
        return pltpu.make_async_copy(
            self.block(chip, self.core), self.mine.at[chip], self.mine_sem.at[chip]
        )

    def hand(self, chip):
        return pltpu.make_async_remote_copy(
            src_ref=self.block(chip, 1 - self.core),
            dst_ref=self.side.at[chip],
            send_sem=self.side_send.at[chip],
            recv_sem=self.side_got.at[chip],
            device_id={"shard": self.z * 2 + 1 - self.core},
            device_id_type=pl.DeviceIdType.MESH,
        )

    def send(self, chip, dst, got, step):
        return pltpu.make_async_remote_copy(
            src_ref=self.stage.at[chip],
            dst_ref=dst.at[chip],
            send_sem=self.sent.at[chip],
            recv_sem=got.at[chip],
            device_id={"shard": (self.z + step) * 2 + self.core},
            device_id_type=pl.DeviceIdType.MESH,
        )

    def to_right(self, chip):
        return self.send(chip, self.from_left, self.left_got, 1)

    def to_left(self, chip):
        return self.send(chip, self.from_right, self.right_got, -1)

    def start(self):
        z, last = self.z, self.chips - 1

        def begin(n, carry):
            chip = jnp.where(z * 2 <= last, last - n, n)
            self.hand(chip).start()
            self.load(chip).start()
            return carry

        lax.fori_loop(0, self.chips, begin, 0)

    def add(self, dst, chip, others):
        size = 32

        def some(n, carry):
            rows = pl.ds(pl.multiple_of(n * size, size), size)
            value = self.mine[chip, rows, :].astype(F32) + self.side[chip, rows, :].astype(F32)
            for other in others:
                value = value + other[chip, rows, :].astype(F32)
            if dst is self.total:
                dst[rows, :] = value
            else:
                dst[chip, rows, :] = value.astype(BF16)
            return carry

        lax.fori_loop(0, self.rows // size, some, 0)

    def ready(self, chip):
        self.load(chip).wait()
        self.hand(chip).wait_recv()

    def step(self, n):
        z, last = self.z, self.chips - 1

        @pl.when((n < last) & (z <= n))
        def _():
            chip = last - n + z
            self.ready(chip)

            @pl.when(z == 0)
            def _():
                self.add(self.stage, chip, ())

            @pl.when(z > 0)
            def _():
                self.to_right(chip).wait_recv()
                self.add(self.stage, chip, (self.from_left,))

            self.to_right(chip).start()

        @pl.when((n < last) & (last - z <= n))
        def _():
            chip = n - last + z
            self.ready(chip)

            @pl.when(z == last)
            def _():
                self.add(self.stage, chip, ())

            @pl.when(z < last)
            def _():
                self.to_left(chip).wait_recv()
                self.add(self.stage, chip, (self.from_right,))

            self.to_left(chip).start()

        @pl.when(n == last)
        def _():
            self.ready(z)

            @pl.when(z == 0)
            def _():
                self.to_left(z).wait_recv()
                self.add(self.total, z, (self.from_right,))

            @pl.when(z == last)
            def _():
                self.to_right(z).wait_recv()
                self.add(self.total, z, (self.from_left,))

            @pl.when((z > 0) & (z < last))
            def _():
                self.to_left(z).wait_recv()
                self.to_right(z).wait_recv()
                self.add(self.total, z, (self.from_left, self.from_right))

            pltpu.make_async_copy(self.total, self.total_hbm, self.total_sem).start()

    def finish(self):
        z = self.z

        def done(chip, carry):
            self.hand(chip).wait_send()

            @pl.when(chip != z)
            def _():
                self.to_right(chip).wait_send()

            return carry

        lax.fori_loop(0, self.chips, done, 0)
        pltpu.make_async_copy(self.total, self.total_hbm, self.total_sem).wait()


FF_TILE = 384


def forward_tiles(rows, buf, weights, ins, outs, acc, part):
    wg, wu, wd = weights
    gate, up, glu = outs
    tiles = wg.shape[0] // FF_TILE
    for t in range(tiles):
        cols = slice(t * FF_TILE, (t + 1) * FF_TILE)
        g = dot(buf[rows, :], wg[cols, :], NT)
        u = dot(buf[rows, :], wu[cols, :], NT)
        act = (gelu_parts(g)[0] * u).astype(BF16)
        gate[rows, cols] = g.astype(BF16)
        up[rows, cols] = u.astype(BF16)
        glu[rows, cols] = act
        more = dot(act, wd[cols, :])
        add_tile(t, tiles, rows, more, acc, part)


def backward_tiles(rows, buf, weights, ins, outs, acc, part):
    wg, wu, wd = weights
    gate, up = ins
    dgate, dup = outs
    tiles = wg.shape[0] // FF_TILE
    for t in range(tiles):
        cols = slice(t * FF_TILE, (t + 1) * FF_TILE)
        d_act = dot(buf[rows, :], wd[cols, :], NT)
        value, slope = gelu_parts(gate[rows, cols].astype(F32))
        dg = (d_act * up[rows, cols].astype(F32) * slope).astype(BF16)
        du = (d_act * value).astype(BF16)
        dgate[rows, cols] = dg
        dup[rows, cols] = du
        more = dot(dg, wg[cols, :]) + dot(du, wu[cols, :])
        add_tile(t, tiles, rows, more, acc, part)


def add_tile(t, tiles, rows, more, acc, part):
    if t == 0:
        acc[...] = more
    elif t < tiles - 1:
        acc[...] += more
    else:
        part[rows, :] = (acc[...] + more).astype(BF16)


def comm_kernel(tiles_of, n_saved, n_made, gathers, sums, bits, *refs):
    refs = list(refs)

    def take(n):
        out = refs[:n]
        del refs[:n]
        return out

    heavy = tiles_of is not None
    own_hbm = take(1)[0] if gathers else None
    loads_from = take(3 + n_saved) if heavy else []
    part_in = take(1)[0] if sums else None
    swap_from = take(len(bits))
    all_hbm = take(1)[0] if gathers else None
    made_hbm = take(n_made + 1) if heavy else []
    total_hbm = take(1)[0] if sums else None
    swap_to = take(len(bits))
    buf = take(1)[0] if gathers else None
    loads_to = take(3 + n_saved) if heavy else []
    made = take(n_made + 1) if heavy else []
    acc = take(1)[0] if heavy else None
    total = take(1)[0] if sums else None
    chain_bufs = take(5) if sums else None
    line_sems = take(6) if gathers else None
    chain_sems = take(7) if sums else None
    out_sem = take(1)[0] if gathers else None
    load_sem = take(1)[0] if heavy else None
    swap_sem = take(1)[0] if bits else None

    chips = lax.axis_size("shard") // 2
    greet_neighbours(chips, sorted(set(bits)))
    swaps = swap_copies(swap_from, swap_to, bits, swap_sem)
    line = chain = None
    if gathers:
        line = Line(own_hbm, buf, line_sems[:5], chips)
        line.start()
        keep = pltpu.make_async_copy(own_hbm, line.place(line.z, line.core), line_sems[5])
        keep.start()
        pair = 2 * own_hbm.shape[0]
    if sums:
        chain = Chain(part_in, total, total_hbm, chain_bufs, chain_sems, chips)
        chain.start()
    for swap in swaps:
        swap.start()
    loads = [
        pltpu.make_async_copy(src, dst, load_sem.at[n])
        for n, (src, dst) in enumerate(zip(loads_from, loads_to))
    ]
    for load in loads:
        load.start()
    if gathers:
        keep.wait()

    def outs(chip):
        rows = pl.ds(pl.multiple_of(chip * pair, pair), pair)
        return [
            pltpu.make_async_copy(src.at[rows], dst.at[rows], out_sem.at[n, chip])
            for n, (src, dst) in enumerate(zip([buf] + made, [all_hbm] + made_hbm))
        ]

    def step(n, carry):
        if gathers:
            line.pass_on(n)
        if sums and gathers:

            @pl.when(n > 0)
            def _():
                chain.step(n - 1)

        elif sums:
            chain.step(n)
        if gathers:
            chip = line.chip_at(n)
            line.wait_side(chip)
            rows = pl.ds(pl.multiple_of(chip * pair, pair), pair)
            if heavy:

                @pl.when(n == 0)
                def _():
                    for load in loads:
                        load.wait()

                tiles_of(rows, buf, loads_to[:3], loads_to[3:], made[:-1], acc, made[-1])
            for copy in outs(chip):
                copy.start()
        return carry

    lax.fori_loop(0, chips, step, 0)
    if sums and gathers:
        chain.step(chips - 1)
    if sums:
        chain.finish()
    if gathers:
        line.finish()

        def drain(chip, carry):
            for copy in outs(chip):
                copy.wait()
            return carry

        lax.fori_loop(0, chips, drain, 0)
    for swap in swaps:
        swap.wait()


def comm_call(
    number, own=None, part=None, tiles_of=None, weights=(), saved=(), n_made=0, swaps=()
):
    shards = lax.axis_size("shard")
    chips = shards // 2
    gathers, sums, heavy = own is not None, part is not None, tiles_of is not None
    ins, outs, scratch, sems = [], [], [], []
    width = own.shape[1] if gathers else part.shape[1]
    flops = 0
    moved = 0
    if gathers:
        rows = own.shape[0] * shards
        wide = jax.ShapeDtypeStruct((rows, width), BF16)
        ins.append(own)
        outs.append(wide)
        scratch.append(pltpu.VMEM((rows, width), BF16))
        moved += 30 * rows * width
    if heavy:
        ins += list(weights) + list(saved)
        units = weights[0].shape[0]
        thin = jax.ShapeDtypeStruct((rows, units), BF16)
        outs += [thin] * n_made + [wide]
        scratch += [pltpu.VMEM(x.shape, BF16) for x in ins[1:]]
        scratch += [pltpu.VMEM((rows, units), BF16)] * n_made
        scratch += [pltpu.VMEM((rows, width), BF16)]
        scratch += [pltpu.VMEM((2 * own.shape[0], width), F32)]
        flops = 6 * rows * units * width
    if sums:
        ins.append(part)
        size = part.shape[0] // shards
        outs.append(jax.ShapeDtypeStruct((size, width), F32))
        scratch.append(pltpu.VMEM((size, width), F32))
        scratch += [pltpu.VMEM((chips, size, width), BF16)] * 5
        moved += 30 * part.shape[0] * width
    dma = pltpu.SemaphoreType.DMA
    bits = tuple(bit for _, bit in swaps)
    ins += [x for x, _ in swaps]
    outs += [jax.ShapeDtypeStruct(x.shape, x.dtype) for x, _ in swaps]
    if gathers:
        sems += [dma((chips,))] * 5 + [dma]
    if sums:
        sems += [dma((chips,))] * 6 + [dma]
    if gathers:
        sems.append(dma((n_made + 2 if heavy else 1, chips)))
    if heavy:
        sems.append(dma((3 + len(saved),)))
    if bits:
        sems.append(dma((2, len(bits))))
    kernel = functools.partial(comm_kernel, tiles_of, len(saved), n_made, gathers, sums, bits)
    return pl.pallas_call(
        kernel,
        in_specs=[ANYWHERE] * len(ins),
        out_specs=[ANYWHERE] * len(outs),
        out_shape=outs,
        scratch_shapes=scratch + sems,
        compiler_params=pltpu.CompilerParams(
            collective_id=number, has_side_effects=True, vmem_limit_bytes=58 * 1024 * 1024
        ),
        cost_estimate=pl.CostEstimate(flops=flops, bytes_accessed=moved, transcendentals=0),
        name="comm%d" % number,
    )(*ins)


class Stream:
    def __init__(self, src, final, axis, bits, bufs, sems, dealt=None):
        self.src, self.final, self.axis, self.bits = src, final, axis, bits
        self.kept, self.first, self.half_sum, self.second, self.quarter_sum = bufs
        self.send, self.got, self.local = sems
        self.dealt = self.quarter_sum if dealt is None else dealt
        r = lax.axis_index("replica")
        self.b1, self.b2 = (lax.rem(r // bit, 2) for bit in bits)
        self.half = src.shape[axis] // 2
        self.quarter = self.half // 2

    def cut(self, ref, start, size):
        return ref.at[(slice(None),) * self.axis + (pl.ds(start, size),)]

    def copy(self, n, src, dst, bit):
        return pltpu.make_async_remote_copy(
            src_ref=src,
            dst_ref=dst,
            send_sem=self.send.at[n],
            recv_sem=self.got.at[n],
            device_id={"replica": flipped(bit)},
            device_id_type=pl.DeviceIdType.MESH,
        )

    def exchange(self, n):
        half, quarter = self.half, self.quarter
        own = self.b1 * half + self.b2 * quarter
        if n == 0:
            return self.copy(0, self.cut(self.src, (1 - self.b1) * half, half), self.first, self.bits[0])
        if n == 1:
            part = self.cut(self.half_sum, (1 - self.b2) * quarter, quarter)
            return self.copy(1, part, self.second, self.bits[1])
        if n == 2:
            return self.copy(2, self.dealt, self.cut(self.final, own, quarter), self.bits[1])
        part = self.cut(self.final, self.b1 * half, half)
        return self.copy(3, part, part, self.bits[0])

    def arrived(self, n):
        if n < 2:
            return self.exchange(n)
        other = 1 - self.b2 if n == 2 else self.b2
        if n == 2:
            place = self.cut(self.final, self.b1 * self.half + other * self.quarter, self.quarter)
            return self.copy(2, self.dealt, place, self.bits[1])
        place = self.cut(self.final, (1 - self.b1) * self.half, self.half)
        return self.copy(3, place, place, self.bits[0])

    def load(self):
        return pltpu.make_async_copy(
            self.cut(self.src, self.b1 * self.half, self.half), self.kept, self.local.at[0]
        )

    def settle(self):
        own = self.b1 * self.half + self.b2 * self.quarter
        return pltpu.make_async_copy(
            self.dealt, self.cut(self.final, own, self.quarter), self.local.at[1]
        )

    def start(self):
        self.exchange(0).start()
        self.load().start()

    def add_first(self):
        self.load().wait()
        self.exchange(0).wait_recv()
        add_into(self.half_sum, self.kept, self.first)
        self.exchange(1).start()

    def add_second(self):
        self.exchange(1).wait_recv()
        add_into(
            self.quarter_sum, self.cut(self.half_sum, self.b2 * self.quarter, self.quarter), self.second
        )

    def give_back(self):
        self.exchange(2).start()
        self.settle().start()

    def give_half(self):
        self.settle().wait()
        self.arrived(2).wait_recv()
        self.exchange(3).start()

    def finish(self):
        self.arrived(3).wait_recv()
        for n in range(4):
            self.exchange(n).wait_send()


def add_into(dst, a, b):
    size = 1 if len(dst.shape) == 4 else 32

    def some(n, carry):
        rows = pl.ds(pl.multiple_of(n * size, size), size)
        dst[rows] = (a[rows].astype(F32) + b[rows].astype(F32)).astype(BF16)
        return carry

    lax.fori_loop(0, dst.shape[0] // size, some, 0)


def tail_kernel(
    part_in, head_a, head_b, out_a, out_b,
    total_hbm, final_a, final_b, final_c, final_d,
    *refs,
):
    refs = list(refs)

    def take(n):
        out = refs[:n]
        del refs[:n]
        return out

    (total,) = take(1)
    chain_bufs = take(5)
    stream_bufs = [take(5) for _ in range(4)]
    dealt = take(2)
    chain_sems = take(7)
    stream_sems = [take(3) for _ in range(4)]
    deal_send, deal_got, deal_local = take(3)
    shards = lax.axis_size("shard")
    chips = shards // 2
    me = lax.axis_index("shard")
    barrier = pltpu.get_barrier_semaphore()
    peers = [lax.rem(me + n, shards) for n in range(1, shards)]
    for peer in peers:
        pl.semaphore_signal(
            barrier, inc=1, device_id={"shard": peer}, device_id_type=pl.DeviceIdType.MESH
        )
    for bit in (1, 2):
        pl.semaphore_signal(
            barrier,
            inc=1,
            device_id={"replica": flipped(bit)},
            device_id_type=pl.DeviceIdType.MESH,
        )
    pl.semaphore_wait(barrier, shards - 1 + 2)
    streams = [
        Stream(src, final, axis, bits, bufs, sems, target)
        for src, final, axis, bits, bufs, sems, target in zip(
            (head_a, head_b, out_a, out_b),
            (final_a, final_b, final_c, final_d),
            (1, 1, 0, 0),
            ((1, 2), (2, 1), (2, 1), (1, 2)),
            stream_bufs,
            stream_sems,
            (dealt[0], dealt[1], None, None),
        )
    ]
    for stream in streams:
        stream.start()
    chain = Chain(part_in, total, total_hbm, chain_bufs, chain_sems, chips)
    chain.start()

    def deal(k, peer, src, n):
        return pltpu.make_async_remote_copy(
            src_ref=streams[k].quarter_sum.at[peer],
            dst_ref=dealt[k].at[src],
            send_sem=deal_send.at[k, n],
            recv_sem=deal_got.at[k, src],
            device_id={"shard": peer},
            device_id_type=pl.DeviceIdType.MESH,
        )

    def own_deal(k):
        return pltpu.make_async_copy(
            streams[k].quarter_sum.at[me], dealt[k].at[me], deal_local.at[k]
        )

    chain.step(0)
    for stream in streams:
        stream.add_first()
    chain.step(1)
    for stream in streams:
        stream.add_second()
    for k in range(2):
        for n, peer in enumerate(peers):
            deal(k, peer, me, n).start()
        own_deal(k).start()
    for stream in streams[2:]:
        stream.give_back()
    chain.step(2)
    for k in range(2):
        own_deal(k).wait()
        for n, peer in enumerate(peers):
            deal(k, me, peer, n).wait_recv()
        streams[k].give_back()
    for stream in streams[2:]:
        stream.give_half()
    for stream in streams[:2]:
        stream.give_half()
    chain.step(3)
    chain.finish()
    for stream in streams:
        stream.finish()
    for k in range(2):
        for n, peer in enumerate(peers):
            deal(k, peer, me, n).wait_send()


def tail_call(number, part, head_a, head_b, out_a, out_b):
    shards = lax.axis_size("shard")
    chips = shards // 2
    width = part.shape[1]
    size = part.shape[0] // shards
    dma = pltpu.SemaphoreType.DMA
    streams = (head_a, head_b, out_a, out_b)
    scratch = [pltpu.VMEM((size, width), F32)] + [pltpu.VMEM((chips, size, width), BF16)] * 5

    def scaled(x, axis, by):
        shape = list(x.shape)
        shape[axis] //= by
        return pltpu.VMEM(tuple(shape), BF16)

    for x, axis in zip(streams, (1, 1, 0, 0)):
        scratch += [scaled(x, axis, 2)] * 3 + [scaled(x, axis, 4)] * 2
    scratch += [scaled(head_a, 1, 4), scaled(head_b, 1, 4)]
    sems = [dma((chips,))] * 6 + [dma]
    for _ in streams:
        sems += [dma((4,)), dma((4,)), dma((2,))]
    sems += [dma((2, shards - 1)), dma((2, shards)), dma((2,))]
    return pl.pallas_call(
        tail_kernel,
        in_specs=[ANYWHERE] * 5,
        out_specs=[ANYWHERE] * 5,
        out_shape=[jax.ShapeDtypeStruct((size, width), F32)]
        + [jax.ShapeDtypeStruct(x.shape, BF16) for x in streams],
        scratch_shapes=scratch + sems,
        compiler_params=pltpu.CompilerParams(
            collective_id=number, has_side_effects=True, vmem_limit_bytes=56 * 1024 * 1024
        ),
        cost_estimate=pl.CostEstimate(
            flops=0, bytes_accessed=30 * part.shape[0] * width, transcendentals=0
        ),
        name="tail",
    )(part, *streams)


ROW_TILE = 8


def head_kernel(
    own_hbm, sent_hbm, all_hbm, weights_hbm, gains_hbm, buf, got,
    right, left, side, got_line, got_side, keep_sem,
    deal_send, deal_got, spread_send, spread_got, out_sem, local,
):
    shards = lax.axis_size("shard")
    replicas = lax.axis_size("replica")
    chips = shards // 2
    me, r = lax.axis_index("shard"), lax.axis_index("replica")
    tiles = got.shape[1] - 1
    barrier = pltpu.get_barrier_semaphore()
    shard_peers = [lax.rem(me + n, shards) for n in range(1, shards)]
    replica_peers = [lax.rem(r + n, replicas) for n in range(1, replicas)]
    for peer in shard_peers:
        pl.semaphore_signal(
            barrier, inc=1, device_id={"shard": peer}, device_id_type=pl.DeviceIdType.MESH
        )
    for peer in replica_peers:
        pl.semaphore_signal(
            barrier, inc=1, device_id={"replica": peer}, device_id_type=pl.DeviceIdType.MESH
        )
    pl.semaphore_wait(barrier, shards + replicas - 2)

    def deal(peer, src, n):
        return pltpu.make_async_remote_copy(
            src_ref=sent_hbm.at[peer],
            dst_ref=got.at[src],
            send_sem=deal_send.at[n],
            recv_sem=deal_got.at[src],
            device_id={"shard": peer},
            device_id_type=pl.DeviceIdType.MESH,
        )

    for n, peer in enumerate(shard_peers):
        deal(peer, me, n).start()
    mine = pltpu.make_async_copy(sent_hbm.at[me], got.at[me], local.at[0])
    mine.start()
    line = Line(own_hbm, buf, (right, left, side, got_line, got_side), chips)
    line.start()
    keep = pltpu.make_async_copy(own_hbm, line.place(line.z, line.core), keep_sem)
    keep.start()
    mine.wait()
    for n, peer in enumerate(shard_peers):
        deal(me, peer, n).wait_recv()

    def spread(peer, src, n):
        return pltpu.make_async_remote_copy(
            src_ref=got.at[:, pl.ds(0, tiles)],
            dst_ref=weights_hbm.at[:, pl.ds(src * tiles, tiles)],
            send_sem=spread_send.at[n],
            recv_sem=spread_got.at[src],
            device_id={"replica": peer},
            device_id_type=pl.DeviceIdType.MESH,
        )

    for n, peer in enumerate(replica_peers):
        spread(peer, r, n).start()
    own_part = pltpu.make_async_copy(
        got.at[:, pl.ds(0, tiles)], weights_hbm.at[:, pl.ds(r * tiles, tiles)], local.at[1]
    )
    own_part.start()
    gain_part = pltpu.make_async_copy(got.at[:, tiles], gains_hbm, local.at[2])
    gain_part.start()
    keep.wait()
    pair = 2 * own_hbm.shape[0]

    def out(chip):
        rows = pl.ds(pl.multiple_of(chip * pair, pair), pair)
        return pltpu.make_async_copy(buf.at[rows], all_hbm.at[rows], out_sem.at[chip])

    def step(n, carry):
        line.pass_on(n)
        chip = line.chip_at(n)
        line.wait_side(chip)
        out(chip).start()
        return carry

    lax.fori_loop(0, chips, step, 0)
    line.finish()
    for n, peer in enumerate(shard_peers):
        deal(peer, me, n).wait_send()
    for n, peer in enumerate(replica_peers):
        spread(peer, r, n).wait_send()
        spread(r, peer, n).wait_recv()
    own_part.wait()
    gain_part.wait()

    def drain(chip, carry):
        out(chip).wait()
        return carry

    lax.fori_loop(0, chips, drain, 0)


def head_call(number, own, sent):
    shards = lax.axis_size("shard")
    replicas = lax.axis_size("replica")
    chips = shards // 2
    size, width = own.shape
    tiles, cols = sent.shape[1] - 1, sent.shape[3]
    dma = pltpu.SemaphoreType.DMA
    return pl.pallas_call(
        head_kernel,
        in_specs=[ANYWHERE] * 2,
        out_specs=[ANYWHERE] * 3,
        out_shape=[
            jax.ShapeDtypeStruct((size * shards, width), BF16),
            jax.ShapeDtypeStruct((shards, tiles * replicas, ROW_TILE, cols), BF16),
            jax.ShapeDtypeStruct((shards, ROW_TILE, cols), BF16),
        ],
        scratch_shapes=[
            pltpu.VMEM((size * shards, width), BF16),
            pltpu.VMEM(sent.shape, BF16),
        ]
        + [dma((chips,))] * 5
        + [dma]
        + [dma((shards - 1,)), dma((shards,)), dma((replicas - 1,)), dma((replicas,))]
        + [dma((chips,)), dma((3,))],
        compiler_params=pltpu.CompilerParams(
            collective_id=number, has_side_effects=True, vmem_limit_bytes=32 * 1024 * 1024
        ),
        cost_estimate=pl.CostEstimate(
            flops=0, bytes_accessed=100 * size * shards * width, transcendentals=0
        ),
        name="head",
    )(own, sent)


def over_tokens_kernel(a0, a1, b0, b1, c0, c1, x0, x1, g0, g1, out_ref):
    i = pl.program_id(0)
    tiles = pl.num_programs(0) // 3

    def product(l0, l1, r0, r1):
        out_ref[...] = (dot(l0[...], r0[...], TN) + dot(l1[...], r1[...], TN)).astype(BF16)

    @pl.when(i < tiles)
    def _():
        product(a0, a1, x0, x1)

    @pl.when((i >= tiles) & (i < 2 * tiles))
    def _():
        product(b0, b1, x0, x1)

    @pl.when(i >= 2 * tiles)
    def _():
        product(c0, c1, g0, g1)


def over_tokens(gates, ups, glus, xs, gs):
    rows, units = glus[0].shape
    width = xs[0].shape[1]
    tiles = units // FF_TILE
    whole = pl.BlockSpec((rows, width), lambda i: (0, 0), pipeline_mode=pl.Buffered(1))

    def some(n):
        return pl.BlockSpec((rows, FF_TILE), lambda i: (0, jnp.clip(i - n * tiles, 0, tiles - 1)))

    return pl.pallas_call(
        over_tokens_kernel,
        grid=(3 * tiles,),
        in_specs=[some(0), some(0), some(1), some(1), some(2), some(2)] + [whole] * 4,
        out_specs=pl.BlockSpec((FF_TILE, width), lambda i: (i, 0)),
        out_shape=jax.ShapeDtypeStruct((3 * units, width), BF16),
        compiler_params=kernel_params(),
        cost_estimate=pl.CostEstimate(
            flops=12 * rows * units * width, bytes_accessed=16 * rows * width, transcendentals=0
        ),
        name="over_tokens",
    )(*gates, *ups, *glus, *xs, *gs)


def swap_cores(x):
    n = lax.axis_size("shard")
    return lax.ppermute(x, "shard", [(s, s ^ 1) for s in range(n)])


def gather(x, axis_name, axis):
    return lax.all_gather(x, axis_name, axis=axis, tiled=True)


def scatter(x, axis_name, axis):
    return lax.psum_scatter(x, axis_name, scatter_dimension=axis, tiled=True)


def partner(x, bit):
    n = lax.axis_size("replica")
    return lax.ppermute(x, "replica", [(r, r ^ bit) for r in range(n)])


def halve_send(x, axis, bit):
    half = x.shape[axis] // 2
    mine = lax.rem(lax.axis_index("replica") // bit, 2)
    kept = lax.dynamic_slice_in_dim(x, mine * half, half, axis)
    sent = lax.dynamic_slice_in_dim(x, (1 - mine) * half, half, axis)
    return kept, partner(sent, bit)


def halve_sum(kept, got):
    return (kept.astype(F32) + got.astype(F32)).astype(BF16)


def halve(x, axis, bit):
    return halve_sum(*halve_send(x, axis, bit))


def join(x, other, axis, bit):
    mine = lax.rem(lax.axis_index("replica") // bit, 2) == 0
    return jnp.concatenate(
        [jnp.where(mine, x, other), jnp.where(mine, other, x)], axis=axis
    )


def double(x, axis, bit):
    return join(x, partner(x, bit), axis, bit)


class ReplicaSum:
    def __init__(self, x):
        half = x.shape[0] // 2
        self.kept = [x[:half], x[half:]]
        self.stage = 0

    def bits(self):
        return (1, 2) if self.stage in (0, 3) else (2, 1)

    def sends(self):
        pairs = []
        for n, bit in enumerate(self.bits()):
            x = self.kept[n]
            if self.stage < 2:
                half = x.shape[0] // 2
                mine = lax.rem(lax.axis_index("replica") // bit, 2)
                self.kept[n] = lax.dynamic_slice_in_dim(x, mine * half, half)
                x = lax.dynamic_slice_in_dim(x, (1 - mine) * half, half)
            pairs.append((x, bit))
        return pairs

    def receive(self, got):
        for n, (bit, other) in enumerate(zip(self.bits(), got)):
            if self.stage < 2:
                self.kept[n] = halve_sum(self.kept[n], other)
            else:
                self.kept[n] = join(self.kept[n], other, 0, bit)
        self.stage += 1

    def permute(self):
        self.receive([partner(x, bit) for x, bit in self.sends()])

    def result(self):
        return jnp.concatenate(self.kept).astype(F32)

    def thirds(self):
        first, second = self.kept
        third = (first.shape[0] + second.shape[0]) // 3
        rest = first.shape[0] - third
        middle = jnp.concatenate([first[third:], second[:rest]])
        return first[:third].astype(F32), middle.astype(F32), second[rest:].astype(F32)


def all_sends(sums):
    return [pair for one in sums for pair in one.sends()]


def all_receive(sums, got):
    for n, one in enumerate(sums):
        one.receive(got[2 * n : 2 * n + 2])


def sum_replicas(x):
    one = ReplicaSum(x)
    for _ in range(4):
        one.permute()
    return one.result()


def exchange(x):
    return lax.all_to_all(x, "shard", 0, 0, tiled=True)


def fast_on_device(
    tokens,
    w_query,
    w_key,
    w_value,
    w_output,
    gain_attn_in,
    gain_attn_out,
    gain_ffn_in,
    gain_ffn_out,
    w_gate,
    w_up,
    w_down,
    segment_ids,
    cotangent,
):
    tok_rows, width = tokens.shape
    w_rows = w_query.shape[0]
    shards = lax.axis_size("shard")
    replicas = lax.axis_size("replica")
    group_rows = tok_rows * shards
    shard_index = lax.axis_index("shard")
    first_core = lax.rem(shard_index, 2) == 0
    piece = w_rows // replicas

    start = lax.axis_index("replica") * piece
    wq = lax.dynamic_slice_in_dim(w_query, start, piece)
    wk = lax.dynamic_slice_in_dim(w_key, start, piece)
    wv = lax.dynamic_slice_in_dim(w_value, start, piece)
    sent = jnp.concatenate(
        [
            wq.reshape(piece, H, 2, 2, QUARTER).swapaxes(2, 3).reshape(piece, H, HD),
            wk.reshape(piece, KV, 2, 2, QUARTER).swapaxes(2, 3).reshape(piece, H, HALF),
            wv.reshape(piece, H, HALF),
        ],
        axis=2,
    ).swapaxes(0, 1)
    cols = 2 * HD
    gain_stack = jnp.stack([gain_attn_in, gain_attn_out, gain_ffn_in, gain_ffn_out])
    own_gains = jnp.pad(gain_stack.reshape(-1), (0, ROW_TILE * cols - gain_stack.size))
    sent = jnp.concatenate(
        [
            sent.reshape(shards, piece // ROW_TILE, ROW_TILE, cols),
            jnp.broadcast_to(own_gains.reshape(1, 1, ROW_TILE, cols), (shards, 1, ROW_TILE, cols)),
        ],
        axis=1,
    )
    x_group, head_w, all_gains = head_call(7, tokens, sent)
    head_w = head_w.reshape(width, cols)
    gains = all_gains.reshape(shards, -1)[:, : gain_stack.size].reshape(shards, 4, w_rows)
    gains = gains.swapaxes(0, 1).reshape(4, width).astype(F32)

    segment_row = segment_ids[0]
    smaller = jnp.sum((segment_row[:, None] < segment_row[None, :]).astype(jnp.int32), axis=0)
    earlier = jnp.concatenate([jnp.zeros((PROMPT,), jnp.int32), PROMPT + smaller])
    index = jnp.arange(group_rows, dtype=jnp.int32)
    low_row = earlier[None, :]
    positions = jnp.where(index < PROMPT, index, index - (earlier - PROMPT))
    rates = THETA ** (-(jnp.arange(HALF, dtype=F32) * 2.0) / HD)
    angles = positions.astype(F32)[:, None] * rates[None, :]
    cosine = jnp.cos(angles)
    sine = jnp.sin(angles)
    table = jnp.concatenate(
        [
            cosine[:, :QUARTER], cosine[:, :QUARTER], -sine[:, :QUARTER], sine[:, :QUARTER],
            cosine[:, QUARTER:], cosine[:, QUARTER:], -sine[:, QUARTER:], sine[:, QUARTER:],
        ],
        axis=1,
    )

    normed, queries, kv_own = qkv_call(x_group, gains[0:1], head_w, table)
    kv_other = swap_cores(kv_own)
    kv_low = jnp.where(first_core, kv_own, kv_other)
    kv_high = jnp.where(first_core, kv_other, kv_own)
    keys = jnp.concatenate([kv_low[:, :HALF], kv_high[:, :HALF]], axis=1)
    values = jnp.concatenate([kv_low[:, HALF:], kv_high[:, HALF:]], axis=1)
    attended, lse, raw_top, raw_end = attend_call(queries, keys, values, low_row, w_output)
    x_float = tokens.astype(F32)
    grad_top = cotangent.astype(F32)
    chunks = 2
    size = tok_rows // chunks

    weights = (w_gate, w_up, w_down)
    (raw_first,) = comm_call(0, part=raw_top)

    def enter(raw, c):
        hidden = x_float[c * size : (c + 1) * size] + rms_scaled(raw, gains[1])
        return hidden, rms_scaled(hidden, gains[2]).astype(BF16)

    def leave(raw, hidden, c):
        out = (hidden + rms_scaled(raw, gains[3])).astype(BF16)
        _, pull = jax.vjp(rms_scaled, raw, gains[3])
        d_raw, gain_term = pull(grad_top[c * size : (c + 1) * size])
        return out, d_raw.astype(BF16), gain_term

    hidden_first, low_first = enter(raw_first, 0)
    normed_0, gate_0, up_0, glu_0, part_0, raw_second = comm_call(
        1, low_first, raw_end, forward_tiles, weights, n_made=3
    )
    hidden_second, low_second = enter(raw_second, 1)
    normed_1, gate_1, up_1, glu_1, part_1, ffn_first = comm_call(
        1, low_second, part_0, forward_tiles, weights, n_made=3
    )
    out_first, d_first, g4_first = leave(ffn_first, hidden_first, 0)
    d_all_0, d_gate_0, d_up_0, d_part_0, ffn_second = comm_call(
        2, d_first, part_1, backward_tiles, weights, (gate_0, up_0), n_made=2
    )
    out_second, d_second, g4_second = leave(ffn_second, hidden_second, 1)
    d_all_1, d_gate_1, d_up_1, d_part_1, d_normed_first = comm_call(
        2, d_second, d_part_0, backward_tiles, weights, (gate_1, up_1), n_made=2
    )
    glus, d_groups = (glu_0, glu_1), (d_all_0, d_all_1)
    d_gates, d_ups, normed_groups = (d_gate_0, d_gate_1), (d_up_0, d_up_1), (normed_0, normed_1)
    hidden_parts, raw_parts = (hidden_first, hidden_second), (raw_first, raw_second)
    outs, gain_four = (out_first, out_second), (g4_first, g4_second)

    ffn_part = over_tokens(d_gates, d_ups, glus, normed_groups, d_groups)
    ffn_sum = lax.psum(ffn_part, "replica")

    def back(d_normed, c):
        rows = slice(c * size, (c + 1) * size)
        _, pull = jax.vjp(rms_scaled, hidden_parts[c], gains[2])
        part, g3 = pull(d_normed)
        d_hidden = grad_top[rows] + part
        _, pull = jax.vjp(rms_scaled, raw_parts[c], gains[1])
        d_raw, g2 = pull(d_hidden)
        return d_hidden, d_raw.astype(BF16), g2, g3

    d_hidden_first, d_attn_first, g2_first, g3_first = back(d_normed_first, 0)
    ffn_part, d_attn_first = lax.optimization_barrier((ffn_part, d_attn_first))
    d_attn_0, d_normed_second = comm_call(3, d_attn_first, d_part_1)
    d_hidden_second, d_attn_second, g2_second, g3_second = back(d_normed_second, 1)
    (d_attn_1,) = comm_call(4, d_attn_second)
    d_hidden = jnp.concatenate([d_hidden_first, d_hidden_second])
    gain_two, gain_three = (g2_first, g2_second), (g3_first, g3_second)
    dq, dk, dv, grad_out = attend_back_call(
        queries, keys, values, low_row, lse, attended, d_attn_0, d_attn_1, w_output, table
    )
    dkv_low = jnp.concatenate([dk[:, :HALF], dv[:, :HALF]], axis=1)
    dkv_high = jnp.concatenate([dk[:, HALF:], dv[:, HALF:]], axis=1)
    dkv_mine = jnp.where(first_core, dkv_low, dkv_high).astype(F32)
    dkv = dkv_mine + swap_cores(jnp.where(first_core, dkv_high, dkv_low)).astype(F32)
    dk_half = dkv[:, :HALF]
    own = jnp.where(first_core, table[:, :HD], table[:, HD:])
    turned = jnp.concatenate([dk_half[:, QUARTER:], dk_half[:, :QUARTER]], axis=1)
    dk_lin = dk_half * own[:, :HALF] - turned * own[:, HALF:]
    d_lin = jnp.concatenate([dq, dk_lin.astype(BF16), dkv[:, HALF:].astype(BF16)], axis=1)
    part = dot(d_lin, head_w, NT).astype(BF16)
    grad_head = dot(normed, d_lin, TN)
    gain_one = jnp.sum(grad_head * head_w.astype(F32), axis=1) / gains[0]
    gain_terms = jnp.stack([gain_one, sum(gain_two), sum(gain_three), sum(gain_four)], axis=1)
    padded = jnp.pad(gain_terms, ((0, 0), (0, HALF - gain_terms.shape[1])))
    cut = HD + HALF
    moved = (shards, w_rows // ROW_TILE, ROW_TILE)
    head_a = grad_head[:, :cut].astype(BF16).reshape(*moved, cut)
    head_b = jnp.concatenate([grad_head[:, cut:], padded], axis=1).astype(BF16).reshape(*moved, HD)
    d_normed, left, right, out_left, out_right = tail_call(
        5, part, head_a, head_b, grad_out[:, : width // 2], grad_out[:, width // 2 :]
    )
    left = left.reshape(shards, w_rows, cut).astype(F32)
    right = right.reshape(shards, w_rows, HD).astype(F32)
    _, pull = jax.vjp(rms_scaled, x_float, gains[0])
    input_grad = d_hidden + pull(d_normed)[0]
    grad_query = (
        left[:, :, :HD].reshape(H, w_rows, 2, 2, QUARTER).transpose(1, 0, 3, 2, 4)
    ).reshape(w_rows, H * HD)
    grad_key = (
        left[:, :, HD:]
        .reshape(KV, 2, w_rows, 2, QUARTER)
        .transpose(2, 0, 3, 1, 4)
        .reshape(w_rows, KV * HD)
    )
    grad_value = right[:, :, :HALF].transpose(1, 0, 2).reshape(w_rows, KV * HD)
    grad_out_proj = jnp.concatenate([out_left, out_right], axis=1).astype(F32)
    units = w_gate.shape[0]
    grad_gate, grad_up, grad_down = (
        ffn_sum[n * units : (n + 1) * units].astype(F32) for n in range(3)
    )
    gain_shares = jnp.sum(right[:, :, HALF : HALF + gain_terms.shape[1]], axis=0).T
    return (
        jnp.concatenate(outs),
        input_grad,
        grad_query,
        grad_key,
        grad_value,
        grad_out_proj,
        gain_shares[0],
        gain_shares[1],
        gain_shares[2],
        gain_shares[3],
        grad_gate,
        grad_up,
        grad_down,
    )


def solution(mesh):
    placed = (
        P(("replica", "shard"), None),
        P("shard", None),
        P("shard", None),
        P("shard", None),
        P("shard", None),
        P("shard"),
        P("shard"),
        P("shard"),
        P("shard"),
        P("shard", None),
        P("shard", None),
        P("shard", None),
        P("replica", None),
        P(("replica", "shard"), None),
    )
    heads_fit = mesh.shape["shard"] == H and H == 2 * KV and mesh.shape["replica"] == 4
    body = fast_on_device if heads_fit else on_device
    return jax.shard_map(
        body,
        mesh=mesh,
        in_specs=placed,
        out_specs=(
            P(("replica", "shard"), None),
            P(("replica", "shard"), None),
            P("shard", None),
            P("shard", None),
            P("shard", None),
            P("shard", None),
            P("shard"),
            P("shard"),
            P("shard"),
            P("shard"),
            P("shard", None),
            P("shard", None),
            P("shard", None),
        ),
        check_vma=False,
    )
```
